32 devices in a mesh: groups: 2 (over y), neuron: 8 (over z, x), token: 2 (over core).
Axes of the slice: x: 2, y: 2, z: 4, core: 2. Of those that a mesh axis runs over, the one named last changes fastest.
Arguments:
- activations: bfloat16 [8192, 114688], P(('groups', 'token'), 'neuron'), parts along dimension 0, as said below
- basis: float32 [229376, 64], P(('groups', 'neuron')), parts along dimension 0, may hold values from -0.015625 to 0.015625
Outputs:
- embedding: float32 [229376, 64], P(('groups', 'neuron')), parts along dimension 0
The draws below stay inside these ranges and needn't reach their ends.
There are 2 independent parts, one for each index of `groups`. The reference program is written for one: setup_inputs(seed, part) draws one part's arguments, and reference() takes and returns one part's arrays. A program takes and returns all parts, laid end to end along the dimension named above; each array names one. Nothing has to cross between parts.
Inputs may be any that keep to these rules, and one draw needn't show every extreme that they name: Finite real activations whose neurons differ in mean and scale.
All inputs are finite; a program needn't handle non-finite values.
Results may differ from the reference program's by a relative error of at most 0.0043.
Values may be sent and summed in bfloat16 or wider, within the bound.
No kernel may reach another device: no remote copies, remote signals or barrier semaphores. Data moves between devices by JAX's collectives and lax.ppermute only.
A program may use at most 192 MiB of HBM per device.

```python
import jax
import jax.numpy as jnp
from jax import lax

K = 64
NEURONS = 114688
TOKENS = 4096


def draw_activations(key, part):
    keys = jax.random.split(key, 6)
    col_scale = jnp.exp(jax.random.uniform(keys[0], (NEURONS,), jnp.float32, 0.0, 2.302585))
    row_scale = jnp.exp(jax.random.uniform(keys[1], (TOKENS,), jnp.float32, 0.0, 2.302585))
    token_factor = jax.random.normal(keys[2], (TOKENS,), jnp.float32)
    neuron_factor = jax.random.normal(keys[3], (NEURONS,), jnp.float32)
    col_mean = jax.random.normal(keys[4], (NEURONS,), jnp.float32)
    noise = jax.random.normal(keys[5], (TOKENS, NEURONS), jnp.float32)
    shared = 0.2
    inner = row_scale[:, None] * noise + shared * token_factor[:, None] * neuron_factor[None, :]
    values = col_mean[None, :] + col_scale[None, :] * inner
    return values.astype(jnp.bfloat16)


def steps_of(own_key, extent, cuts, smallest, high):
    factor_of, own = 1.0, jax.random.fold_in(own_key, 6)
    for axis_at, shards_of in cuts:
        steps = jnp.exp(jax.random.uniform(jax.random.fold_in(own, axis_at), (shards_of,), jnp.float32, smallest / len(cuts), high / len(cuts)))
        factor_of = factor_of * jnp.repeat(steps, extent[axis_at] // shards_of).reshape([-1 if axis == axis_at else 1 for axis in range(len(extent))])
    return factor_of


def scatter_about(stream_key, shape, spread, most, pieces=(), dtype=jnp.bfloat16):
    loudness = steps_of(stream_key, shape, pieces, -0.22, 0.18) if pieces else 1.0
    result = jax.random.normal(stream_key, shape, jnp.float32) * spread * loudness
    return jnp.minimum(jnp.maximum(result, -most), most).astype(dtype)


def setup_inputs(seed: int = 0, part: int = 0) -> dict:
    streams_of = jax.random.split(jax.random.key(seed), 3)
    own_keys = jax.random.split(jax.random.fold_in(streams_of[2], part), 3)
    return {
        "activations": draw_activations(jax.random.fold_in(jax.random.fold_in(streams_of[2], part), 71), part),
        "basis": scatter_about(own_keys[1], (NEURONS, K), NEURONS ** -0.5, 0.015625, ((0, 8),), jnp.float32),
    }


def reference(activations, basis):
    tokens = activations.shape[0]
    col_sum = lax.optimization_barrier(jnp.sum(activations.astype(jnp.float32), axis=0))
    col_sq = lax.optimization_barrier(jnp.sum(jnp.square(activations.astype(jnp.float32)), axis=0))
    col_mean = col_sum / tokens
    col_scale = lax.rsqrt(col_sq / tokens - col_mean * col_mean + 1e-05)
    scaled = (col_scale[:, None] * basis).astype(jnp.bfloat16)
    offset = jnp.dot(col_mean[None, :], scaled.astype(jnp.float32), precision=lax.Precision.HIGHEST)
    projection = (jnp.dot(activations.astype(jnp.float32), scaled.astype(jnp.float32), preferred_element_type=jnp.float32) - offset).astype(jnp.bfloat16)
    cross = lax.dot_general(activations.astype(jnp.float32), projection.astype(jnp.float32), (((0,), (0,)), ((), ())), preferred_element_type=jnp.float32)
    proj_sum = lax.optimization_barrier(jnp.sum(projection.astype(jnp.float32), axis=0))
    weighted = (cross - col_mean[:, None] * proj_sum[None, :]) * col_scale[:, None] / tokens
    gram = jnp.einsum('nk,nl->kl', weighted, weighted, precision=lax.Precision.HIGHEST) / NEURONS
    lower = jnp.linalg.cholesky(gram)
    solved = jax.scipy.linalg.solve_triangular(lower, weighted.T, lower=True)
    return solved.T
```

```python
import jax
import jax.numpy as jnp
from jax import lax
from jax.sharding import PartitionSpec as P

NEURONS = 114688
F32 = jnp.float32
BF16 = jnp.bfloat16
HIGHEST = lax.Precision.HIGHEST


def token_sum(x, m):
    if m == 2:
        return x + lax.ppermute(x, "token", [(0, 1), (1, 0)])
    return lax.psum(x, "token")


def gather_blocks(x, n):
    return lax.all_to_all(jnp.broadcast_to(x[None], (n,) + x.shape), "neuron", 0, 0)


def local(activations, basis):
    tok_dev, neu_dev = activations.shape
    n, m = lax.axis_size("neuron"), lax.axis_size("token")
    tokens = tok_dev * m
    cols = basis.shape[1]
    basis_t = basis.T
    col_sum = jnp.sum(activations.astype(F32), axis=0)
    col_sq = jnp.sum(jnp.square(activations.astype(F32)), axis=0)
    sums = token_sum(jnp.stack([col_sum, col_sq]), m)
    col_mean = sums[0:1] / tokens
    col_scale = lax.rsqrt(sums[1:2] / tokens - col_mean * col_mean + 1e-05)
    scaled = (col_scale * basis_t).astype(BF16)
    offset = jnp.sum(scaled.astype(F32) * col_mean, axis=1, keepdims=True)
    part = lax.dot_general(
        scaled, activations, (((1,), (1,)), ((), ())), preferred_element_type=F32
    ) - offset
    blocks = part.astype(BF16).reshape(cols, n, tok_dev // n).transpose(1, 0, 2)
    blocks = lax.all_to_all(blocks, "neuron", 0, 0)
    own = jnp.sum(blocks.astype(F32), axis=0).astype(BF16)
    proj = gather_blocks(own, n).transpose(1, 0, 2).reshape(cols, tok_dev)
    cross = lax.dot_general(
        proj, activations, (((1,), (0,)), ((), ())), preferred_element_type=F32
    )
    proj_sum = jnp.sum(proj.astype(F32), axis=1, keepdims=True)
    summed = token_sum(cross - proj_sum * col_mean, m)
    weighted = summed * col_scale / tokens
    gram_part = lax.dot_general(
        weighted, weighted, (((1,), (1,)), ((), ())), precision=HIGHEST, preferred_element_type=F32
    )
    gram = jnp.sum(gather_blocks(gram_part, n), axis=0) / NEURONS
    lower = jnp.linalg.cholesky(gram)
    solved = jax.scipy.linalg.solve_triangular(lower, weighted, lower=True)
    return solved.T


def solution(mesh):
    placed = (P(("groups", "token"), "neuron"), P(("groups", "neuron"), None))
    return jax.shard_map(
        local, mesh=mesh, in_specs=placed, out_specs=P(("groups", "neuron"), None), check_vma=False
    )
```

```python
import functools

import jax
import jax.numpy as jnp
from jax import lax
from jax.experimental import pallas as pl
from jax.experimental.pallas import tpu as pltpu
from jax.sharding import PartitionSpec as P

NEURONS = 114688
F32 = jnp.float32
BF16 = jnp.bfloat16
MIB = 1 << 20
NT = (((1,), (1,)), ((), ()))


def block_of(size, most):
    return max(b for b in range(128, most + 1, 128) if size % b == 0)


def swap_tokens(x):
    return lax.ppermute(x, "token", [(0, 1), (1, 0)])


def token_sum(x, m):
    return x + swap_tokens(x) if m == 2 else lax.psum(x, "token")


def halves(x):
    head = x.astype(BF16)
    return head, (x - head.astype(F32)).astype(BF16)


def cross_kernel(blocks, proj_ref, act_ref, mean_ref, out_ref, sum_ref):
    j = pl.program_id(0)
    proj = proj_ref[0]
    part = jnp.sum(proj.astype(F32), axis=1, keepdims=True)
    prod = jnp.dot(proj, act_ref[...], preferred_element_type=F32)

    @pl.when(j == 0)
    def _():
        out_ref[...] = prod
        sum_ref[:, 0:1] = part

    @pl.when(j > 0)
    def _():
        out_ref[...] += prod
        sum_ref[:, 0:1] += part

    @pl.when(j == blocks - 1)
    def _():
        out_ref[...] -= sum_ref[:, 0:1] * mean_ref[...]


def cross_slab(proj, act, mean, slab, width):
    blocks, cols, tb = proj.shape
    return pl.pallas_call(
        functools.partial(cross_kernel, blocks),
        grid=(blocks,),
        in_specs=[
            pl.BlockSpec((1, cols, tb), lambda j: (j, 0, 0)),
            pl.BlockSpec((tb, width), lambda j: (j, slab)),
            pl.BlockSpec((1, width), lambda j: (0, slab)),
        ],
        out_specs=pl.BlockSpec((cols, width), lambda j: (0, 0)),
        out_shape=jax.ShapeDtypeStruct((cols, width), F32),
        scratch_shapes=[pltpu.VMEM((cols, 128), F32)],
        compiler_params=pltpu.CompilerParams(vmem_limit_bytes=32 * MIB),
        cost_estimate=pl.CostEstimate(
            flops=2 * blocks * tb * cols * width,
            bytes_accessed=2 * blocks * tb * width,
            transcendentals=0,
        ),
        name="cross",
    )(proj, act, mean)


def combine_kernel(steps, last, tokens, own_ref, got_ref, scale_ref, *refs):
    i = pl.program_id(0)
    if last:
        prev_ref, _, out_ref, gram_ref, acc_ref = refs
    else:
        out_ref, gram_ref, acc_ref = refs
    cols = own_ref.shape[0]
    weighted = (own_ref[...] + got_ref[...]) * scale_ref[...] / tokens
    out_ref[...] = weighted
    both = jnp.concatenate(halves(weighted), axis=0)
    square = lax.dot_general(both, both, NT, preferred_element_type=F32)

    @pl.when(i == 0)
    def _():
        acc_ref[...] = square

    @pl.when(i > 0)
    def _():
        acc_ref[...] += square

    @pl.when(i == steps - 1)
    def _():
        full = acc_ref[...]
        gram = (full[:cols, :cols] + full[cols:, cols:]) + (full[:cols, cols:] + full[cols:, :cols])
        packed = jnp.concatenate([gram[: cols // 2], gram[cols // 2 :]], axis=1)
        if last:
            packed = packed + prev_ref[...]
            for r in range(gram_ref.shape[0]):
                gram_ref[r] = packed
        else:
            gram_ref[...] = packed


def combine_slab(own, got, scale, slab, slabs, tokens, n, prev, buffer):
    cols, width = own.shape
    last = slab == slabs - 1
    nb = block_of(width, 2048)
    steps = width // nb
    here = pl.BlockSpec((cols, nb), lambda i: (0, i))
    there = pl.BlockSpec((cols, nb), lambda i: (0, i + slab * steps))
    packed = (n, cols // 2, 2 * cols) if last else (cols // 2, 2 * cols)
    in_specs = [here, here, pl.BlockSpec((1, nb), lambda i: (0, i + slab * steps))]
    args = [own, got, scale]
    aliases = {}
    if last:
        in_specs += [pl.BlockSpec((cols // 2, 2 * cols), lambda i: (0, 0)), pl.BlockSpec(memory_space=pl.ANY)]
        args += [prev, buffer]
        aliases = {4: 0}
    return pl.pallas_call(
        functools.partial(combine_kernel, steps, last, tokens),
        grid=(steps,),
        in_specs=in_specs,
        out_specs=[there, pl.BlockSpec(packed, lambda i: (0,) * len(packed))],
        out_shape=[
            jax.ShapeDtypeStruct((cols, width * slabs), F32),
            jax.ShapeDtypeStruct(packed, F32),
        ],
        scratch_shapes=[pltpu.VMEM((2 * cols, 2 * cols), F32)],
        input_output_aliases=aliases,
        compiler_params=pltpu.CompilerParams(vmem_limit_bytes=32 * MIB),
        cost_estimate=pl.CostEstimate(
            flops=8 * cols * cols * width, bytes_accessed=12 * cols * width, transcendentals=0
        ),
        name="combine",
    )(*args)


def finish_kernel(gram_ref, weighted_ref, out_ref, inv_ref):
    cols = weighted_ref.shape[0]

    @pl.when(pl.program_id(0) == 0)
    def _():
        packed = jnp.sum(gram_ref[...], axis=0) / NEURONS
        gram = jnp.concatenate([packed[:, :cols], packed[:, cols:]], axis=0)
        row = lax.broadcasted_iota(jnp.int32, (cols, cols), 0)
        lane = lax.broadcasted_iota(jnp.int32, (cols, cols), 1)
        wide = jnp.concatenate([gram, (row == lane).astype(F32)], axis=1)
        tall = [wide[8 * b : 8 * b + 8] for b in range(cols // 8)]
        within = lax.broadcasted_iota(jnp.int32, (8, 1), 0)
        for k in range(cols):
            at, inner = divmod(k, 8)
            pivot_row = tall[at][inner : inner + 1]
            pivot_row = pivot_row / pivot_row[:, k : k + 1]
            for b in range(at, cols // 8):
                factor = tall[b][:, k : k + 1]
                if b == at:
                    factor = jnp.where(within > inner, factor, 0.0)
                tall[b] = tall[b] - factor * pivot_row
        wide = jnp.concatenate(tall, axis=0)
        diag = jnp.sum(jnp.where(row == lane, wide[:, :cols], 0.0), axis=1, keepdims=True)
        head, rest = halves(wide[:, cols:] * lax.rsqrt(diag))
        inv_ref[...] = jnp.concatenate([head, head, rest], axis=1)

    head, rest = halves(weighted_ref[...])
    out_ref[...] = jnp.dot(
        inv_ref[...], jnp.concatenate([head, rest, head], axis=0), preferred_element_type=F32
    )


def finish(grams, weighted):
    cols, width = weighted.shape
    nb = block_of(width, 3584)
    return pl.pallas_call(
        finish_kernel,
        grid=(width // nb,),
        in_specs=[
            pl.BlockSpec(grams.shape, lambda i: (0, 0, 0)),
            pl.BlockSpec((cols, nb), lambda i: (0, i)),
        ],
        out_specs=pl.BlockSpec((cols, nb), lambda i: (0, i)),
        out_shape=jax.ShapeDtypeStruct((cols, width), F32),
        scratch_shapes=[pltpu.VMEM((cols, 3 * cols), BF16)],
        compiler_params=pltpu.CompilerParams(vmem_limit_bytes=32 * MIB),
        name="finish",
    )(grams, weighted)


def local(activations, basis):
    tok_dev, neu_dev = activations.shape
    n, m = lax.axis_size("neuron"), lax.axis_size("token")
    tokens = tok_dev * m
    cols = basis.shape[1]
    basis_t = basis.T
    col_sum = jnp.sum(activations.astype(F32), axis=0)
    col_sq = jnp.sum(jnp.square(activations.astype(F32)), axis=0)
    sums = token_sum(jnp.stack([col_sum, col_sq]), m)
    col_mean = sums[0:1] / tokens
    col_scale = lax.rsqrt(sums[1:2] / tokens - col_mean * col_mean + 1e-05)
    scaled = (col_scale * basis_t).astype(BF16)
    offset = jnp.sum(scaled.astype(F32) * col_mean, axis=1, keepdims=True)
    part = lax.dot_general(scaled, activations, NT, preferred_element_type=F32) - offset
    blocks = part.astype(BF16).reshape(cols, n, tok_dev // n).transpose(1, 0, 2)
    blocks = lax.all_to_all(blocks, "neuron", 0, 0)
    own = jnp.sum(blocks.astype(F32), axis=0).astype(BF16)
    proj = lax.all_to_all(jnp.broadcast_to(own[None], blocks.shape), "neuron", 0, 0)

    slabs = 2
    width = neu_dev // slabs
    terms, swapped = [], []
    for slab in range(slabs):
        terms.append(cross_slab(proj, activations, col_mean, slab, width))
        swapped.append(swap_tokens(terms[-1]))
    weighted = gram = None
    for slab in range(slabs):
        weighted, gram = combine_slab(
            terms[slab], swapped[slab], col_scale, slab, slabs, tokens, n, gram, weighted
        )
    grams = lax.all_to_all(gram, "neuron", 0, 0)
    return finish(grams, weighted).T


def solution(mesh):
    placed = (P(("groups", "token"), "neuron"), P(("groups", "neuron"), None))
    return jax.shard_map(
        local, mesh=mesh, in_specs=placed, out_specs=P(("groups", "neuron"), None), check_vma=False
    )
```

```python
import functools

import jax
import jax.numpy as jnp
from jax import lax
from jax.experimental import pallas as pl
from jax.experimental.pallas import tpu as pltpu
from jax.sharding import PartitionSpec as P

NEURONS = 114688
F32 = jnp.float32
BF16 = jnp.bfloat16
MIB = 1 << 20
NT = (((1,), (1,)), ((), ()))
ROWS = 256
CHUNKS = 4
KEEP = 2
DEPTH = 4
DELAY = 1
SCOPED = 6 * MIB


def block_of(size, most):
    return max(b for b in range(128, most + 1, 128) if size % b == 0)


def swap_tokens(x):
    return lax.ppermute(x, "token", [(0, 1), (1, 0)])


def halves(x):
    head = x.astype(BF16)
    return head, (x - head.astype(F32)).astype(BF16)


def stream_kernel(tokens, chunk, loads, at_chunk, starts, *refs):
    projects = at_chunk is not None
    refs = list(refs)
    take = refs.pop
    if loads is not None:
        act_ref = take(0)
    if loads != 0:
        buf_ref = take(0)
    if projects:
        own_ref, got_ref, basis_ref = take(0), take(0), take(0)
        if not starts:
            part_ref = take(0)
    if loads is not None:
        buf_ref, sums_ref = take(0), take(0)
    slots, tok_dev, _ = buf_ref.shape
    rows = tok_dev // ROWS
    if projects:
        proj_ref, stat_ref = take(0), take(0)
    if loads is not None:
        acc_ref, sem = take(0), take(0)
        into = loads % slots
        copies = [
            pltpu.make_async_copy(
                act_ref.at[pl.ds(j * ROWS, ROWS), pl.ds(loads * chunk, chunk)],
                buf_ref.at[into, pl.ds(j * ROWS, ROWS)],
                sem.at[j],
            )
            for j in range(rows)
        ]
        for copy in copies:
            copy.start()
    if projects:
        scaled_ref = take(0)
        held = at_chunk % slots
        sums = own_ref[...] + got_ref[...]
        mean = sums[0:1] / tokens
        scale = lax.rsqrt(sums[1:2] / tokens - mean * mean + 1e-05)
        stat_ref[0:1] = mean
        stat_ref[1:2] = scale
        scaled = (scale * basis_ref[:, at_chunk * chunk : at_chunk * chunk + chunk]).astype(BF16)
        scaled_ref[...] = scaled
        offset = jnp.sum(scaled.astype(F32) * mean, axis=1, keepdims=True)
    for j in range(rows):
        at = slice(j * ROWS, j * ROWS + ROWS)
        if loads is not None:
            copies[j].wait()
            x = buf_ref[into, at, :].astype(F32)
            total = jnp.sum(x.reshape(ROWS // 8, 8, chunk), axis=0)
            square = jnp.sum((x * x).reshape(ROWS // 8, 8, chunk), axis=0)
            if j == 0:
                acc_ref[0:8] = total
                acc_ref[8:16] = square
            else:
                acc_ref[0:8] += total
                acc_ref[8:16] += square
        if projects:
            part = lax.dot_general(
                scaled_ref[...], buf_ref[held, at, :], NT, preferred_element_type=F32
            ) - offset
            if not starts:
                part = part + part_ref[:, at]
            if len(proj_ref.shape) == 3:
                proj_ref[j] = part.astype(BF16)
            else:
                proj_ref[:, at] = part.astype(proj_ref.dtype)
    if loads is not None:
        sums_ref[0:1] = jnp.sum(acc_ref[0:8], axis=0, keepdims=True)
        sums_ref[1:2] = jnp.sum(acc_ref[8:16], axis=0, keepdims=True)


def stream(tokens, n, chunk, act, loads, buf, at, own, got, basis_t, part, last):
    rows, cols = act.shape[0], basis_t.shape[0]
    vmem = pl.BlockSpec(memory_space=pltpu.VMEM)
    args, in_specs, outs, scratch, aliases = [], [], [], [], {}
    if loads is not None:
        args.append(act)
        in_specs.append(pl.BlockSpec(memory_space=pl.ANY))
        outs += [pltpu.VMEM((KEEP, rows, chunk), BF16), jax.ShapeDtypeStruct((2, chunk), F32)]
        scratch += [pltpu.VMEM((16, chunk), F32), pltpu.SemaphoreType.DMA((rows // ROWS,))]
    if loads != 0:
        if loads is not None:
            aliases = {len(args): 0}
        args.append(buf)
        in_specs.append(vmem)
    if at is not None:
        args += [own, got, basis_t]
        in_specs += [vmem] * 3
        if part is not None:
            args.append(part)
            in_specs.append(vmem)
        blocks = last and rows // n == ROWS
        outs += [
            jax.ShapeDtypeStruct((n, cols, ROWS) if blocks else (cols, rows), BF16 if last else F32),
            jax.ShapeDtypeStruct((2, chunk), F32),
        ]
        scratch.append(pltpu.VMEM((cols, chunk), BF16))
    return list(pl.pallas_call(
        functools.partial(stream_kernel, tokens, chunk, loads, at, part is None),
        in_specs=in_specs,
        out_specs=[vmem] * len(outs),
        out_shape=outs,
        scratch_shapes=scratch,
        input_output_aliases=aliases,
        compiler_params=pltpu.CompilerParams(vmem_limit_bytes=SCOPED),
        cost_estimate=pl.CostEstimate(
            flops=8 * rows * chunk * cols, bytes_accessed=2 * rows * chunk, transcendentals=0
        ),
        name="stream",
    )(*args))


def spread_kernel(blocks_ref, out_ref):
    total = jnp.sum(blocks_ref[...].astype(F32), axis=0).astype(BF16)
    for r in range(out_ref.shape[0]):
        out_ref[r] = total


def spread(blocks):
    return pl.pallas_call(
        spread_kernel,
        out_shape=jax.ShapeDtypeStruct(blocks.shape, BF16),
        compiler_params=pltpu.CompilerParams(vmem_limit_bytes=SCOPED),
        name="spread",
    )(blocks)


def cross_kernel(start, sub, proj_ref, act_ref, stats_ref, out_ref, buf_ref, sem):
    depth = buf_ref.shape[0]
    blocks = out_ref.shape[1] // sub
    copies = [
        pltpu.make_async_copy(
            act_ref.at[:, pl.ds(start + s * sub, sub)], buf_ref.at[s % depth], sem.at[s % depth]
        )
        for s in range(blocks)
    ]
    for copy in copies[:depth]:
        copy.start()
    proj = jnp.concatenate([proj_ref[r] for r in range(proj_ref.shape[0])], axis=1)
    total = jnp.sum(proj.astype(F32), axis=1, keepdims=True)
    for s, copy in enumerate(copies):
        here = slice(s * sub, s * sub + sub)
        copy.wait()
        prod = jnp.dot(proj, buf_ref[s % depth], preferred_element_type=F32)
        if s + depth < blocks:
            copies[s + depth].start()
        out_ref[:, here] = prod - total * stats_ref[0:1, here]


def cross(proj, act, stats, start):
    cols, rows = proj.shape[1], act.shape[0]
    width = stats.shape[1]
    sub = block_of(width, 512)
    vmem = pl.BlockSpec(memory_space=pltpu.VMEM)
    return pl.pallas_call(
        functools.partial(cross_kernel, start, sub),
        in_specs=[vmem, pl.BlockSpec(memory_space=pl.ANY), vmem],
        out_specs=vmem,
        out_shape=jax.ShapeDtypeStruct((cols, width), F32),
        scratch_shapes=[pltpu.VMEM((DEPTH, rows, sub), BF16), pltpu.SemaphoreType.DMA((DEPTH,))],
        compiler_params=pltpu.CompilerParams(vmem_limit_bytes=24 * MIB),
        cost_estimate=pl.CostEstimate(
            flops=8 * rows * cols * width, bytes_accessed=2 * rows * width, transcendentals=0
        ),
        name="cross",
    )(proj, act, stats)


def combine_kernel(pieces, first, last, tokens, own_ref, got_ref, stat_ref, *refs):
    i = pl.program_id(0)
    if not first:
        prev_ref, _, *refs = refs
    out_ref, gram_ref, acc_ref = refs
    cols = own_ref.shape[0]
    weighted = (own_ref[...] + got_ref[...]) * stat_ref[1:2] / tokens
    out_ref[...] = weighted
    both = jnp.concatenate(halves(weighted), axis=0)
    square = lax.dot_general(both, both, NT, preferred_element_type=F32)

    @pl.when(i == 0)
    def _():
        acc_ref[...] = square

    @pl.when(i > 0)
    def _():
        acc_ref[...] += square

    @pl.when(i == pieces - 1)
    def _():
        full = acc_ref[...]
        gram = (full[:cols, :cols] + full[cols:, cols:]) + (full[:cols, cols:] + full[cols:, :cols])
        packed = jnp.concatenate([gram[: cols // 2], gram[cols // 2 :]], axis=1)
        if not first:
            packed = packed + prev_ref[...]
        if last:
            for r in range(gram_ref.shape[0]):
                gram_ref[r] = packed
        else:
            gram_ref[...] = packed


def combine(own, got, stats, start, chunk, whole, tokens, n, prev, buffer, last):
    cols = own.shape[0]
    pieces = own.shape[1] // chunk
    first = prev is None
    here = pl.BlockSpec((cols, chunk), lambda i: (0, i))
    there = pl.BlockSpec((cols, chunk), lambda i: (0, i + start // chunk))
    packed = (n, cols // 2, 2 * cols) if last else (cols // 2, 2 * cols)
    in_specs = [here, here, pl.BlockSpec((2, chunk), lambda i: (0, i))]
    args, aliases = [own, got, stats], {}
    if not first:
        in_specs += [pl.BlockSpec((cols // 2, 2 * cols), lambda i: (0, 0)), pl.BlockSpec(memory_space=pl.ANY)]
        args += [prev, buffer]
        aliases = {4: 0}
    return pl.pallas_call(
        functools.partial(combine_kernel, pieces, first, last, tokens),
        grid=(pieces,),
        in_specs=in_specs,
        out_specs=[there, pl.BlockSpec(packed, lambda i: (0,) * len(packed))],
        out_shape=[
            jax.ShapeDtypeStruct((cols, whole), F32),
            jax.ShapeDtypeStruct(packed, F32),
        ],
        scratch_shapes=[pltpu.VMEM((2 * cols, 2 * cols), F32)],
        input_output_aliases=aliases,
        compiler_params=pltpu.CompilerParams(vmem_limit_bytes=12 * MIB),
        cost_estimate=pl.CostEstimate(
            flops=8 * cols * cols * own.shape[1], bytes_accessed=12 * cols * own.shape[1], transcendentals=0
        ),
        name="combine",
    )(*args)


def finish_kernel(gram_ref, weighted_ref, out_ref, inv_ref):
    cols = weighted_ref.shape[0]

    @pl.when(pl.program_id(0) == 0)
    def _():
        packed = jnp.sum(gram_ref[...], axis=0) / NEURONS
        gram = jnp.concatenate([packed[:, :cols], packed[:, cols:]], axis=0)
        row = lax.broadcasted_iota(jnp.int32, (cols, cols), 0)
        lane = lax.broadcasted_iota(jnp.int32, (cols, cols), 1)
        wide = jnp.concatenate([gram, (row == lane).astype(F32)], axis=1)
        tall = [wide[8 * b : 8 * b + 8] for b in range(cols // 8)]
        within = lax.broadcasted_iota(jnp.int32, (8, 1), 0)
        for k in range(cols):
            at, inner = divmod(k, 8)
            pivot_row = tall[at][inner : inner + 1]
            pivot_row = pivot_row / pivot_row[:, k : k + 1]
            for b in range(at, cols // 8):
                factor = tall[b][:, k : k + 1]
                if b == at:
                    factor = jnp.where(within > inner, factor, 0.0)
                tall[b] = tall[b] - factor * pivot_row
        wide = jnp.concatenate(tall, axis=0)
        diag = jnp.sum(jnp.where(row == lane, wide[:, :cols], 0.0), axis=1, keepdims=True)
        head, rest = halves(wide[:, cols:] * lax.rsqrt(diag))
        inv_ref[...] = jnp.concatenate([head, head, rest], axis=1)

    head, rest = halves(weighted_ref[...])
    out_ref[...] = jnp.dot(
        inv_ref[...], jnp.concatenate([head, rest, head], axis=0), preferred_element_type=F32
    )


def finish(grams, weighted):
    cols, width = weighted.shape
    nb = block_of(width, 2048)
    return pl.pallas_call(
        finish_kernel,
        grid=(width // nb,),
        in_specs=[
            pl.BlockSpec(grams.shape, lambda i: (0, 0, 0)),
            pl.BlockSpec((cols, nb), lambda i: (0, i)),
        ],
        out_specs=pl.BlockSpec((cols, nb), lambda i: (0, i)),
        out_shape=jax.ShapeDtypeStruct((cols, width), F32),
        scratch_shapes=[pltpu.VMEM((cols, 3 * cols), BF16)],
        compiler_params=pltpu.CompilerParams(vmem_limit_bytes=8 * MIB),
        name="finish",
    )(grams, weighted)


def local(activations, basis):
    tok_dev, neu_dev = activations.shape
    n, m = lax.axis_size("neuron"), lax.axis_size("token")
    tokens = tok_dev * m
    cols = basis.shape[1]
    basis_t = basis.T
    chunks = next(c for c in (CHUNKS, 7, 2, 1) if neu_dev % (128 * c) == 0)
    chunk = neu_dev // chunks

    own, got, stats = [], [], []
    part = buf = None
    for step in range(chunks + DELAY):
        loads = step if step < chunks else None
        at = step - DELAY if step >= DELAY else None
        sums = (None, None) if at is None else (own[at], got[at])
        results = stream(
            tokens, n, chunk, activations, loads, buf, at, *sums, basis_t, part, at == chunks - 1
        )
        if loads is not None:
            buf = results.pop(0)
            own.append(results.pop(0))
            got.append(swap_tokens(own[-1]))
        if at is not None:
            part = results.pop(0)
            stats.append(results.pop(0))

    blocks = part if part.ndim == 3 else part.reshape(cols, n, tok_dev // n).transpose(1, 0, 2)
    blocks = spread(lax.all_to_all(blocks, "neuron", 0, 0))
    proj = lax.all_to_all(blocks, "neuron", 0, 0)
    if proj.shape[2] % 128:
        proj = proj.transpose(1, 0, 2).reshape(1, cols, tok_dev)

    split = chunks - max(1, chunks // 4)
    spans = [(0, split), (split, chunks)] if split else [(0, chunks)]
    stats = [jnp.concatenate(stats[lo:hi], axis=1) for lo, hi in spans]
    terms = [cross(proj, activations, stat, lo * chunk) for stat, (lo, _) in zip(stats, spans)]
    swapped = [swap_tokens(term) for term in terms]
    weighted = gram = None
    for term, got, stat, (lo, hi) in zip(terms, swapped, stats, spans):
        weighted, gram = combine(
            term, got, stat, lo * chunk, chunk, neu_dev, tokens, n, gram, weighted, hi == chunks
        )
    grams = lax.all_to_all(gram, "neuron", 0, 0)
    return finish(grams, weighted).T


def solution(mesh):
    placed = (P(("groups", "token"), "neuron"), P(("groups", "neuron"), None))
    return jax.shard_map(
        local, mesh=mesh, in_specs=placed, out_specs=P(("groups", "neuron"), None), check_vma=False
    )
```

```python
import functools

import jax
import jax.numpy as jnp
from jax import lax
from jax.experimental import pallas as pl
from jax.experimental.pallas import tpu as pltpu
from jax.sharding import PartitionSpec as P

NEURONS = 114688
F32 = jnp.float32
BF16 = jnp.bfloat16
MIB = 1 << 20
NT = (((1,), (1,)), ((), ()))
ROWS = 256
CHUNKS = 4
KEEP = 2
DEPTH = 4
LANES = 512
DELAY = 1
SCOPED = 6 * MIB


def block_of(size, most):
    return max(b for b in range(128, most + 1, 128) if size % b == 0)


def swap_tokens(x):
    return lax.ppermute(x, "token", [(0, 1), (1, 0)])


def halves(x):
    head = x.astype(BF16)
    return head, (x - head.astype(F32)).astype(BF16)


def stream_kernel(tokens, chunk, loads, at_chunk, starts, *refs):
    projects = at_chunk is not None
    refs = list(refs)
    take = refs.pop
    if loads is not None:
        act_ref = take(0)
    if loads != 0:
        buf_ref = take(0)
    if projects:
        own_ref, got_ref, basis_ref = take(0), take(0), take(0)
        if not starts:
            part_ref = take(0)
    if loads is not None:
        buf_ref, sums_ref = take(0), take(0)
    slots, tok_dev, _ = buf_ref.shape
    rows = tok_dev // ROWS
    if projects:
        proj_ref, stat_ref = take(0), take(0)
    if loads is not None:
        acc_ref, sem = take(0), take(0)
        into = loads % slots
        copies = [
            pltpu.make_async_copy(
                act_ref.at[pl.ds(j * ROWS, ROWS), pl.ds(loads * chunk, chunk)],
                buf_ref.at[into, pl.ds(j * ROWS, ROWS)],
                sem.at[j],
            )
            for j in range(rows)
        ]
        for copy in copies:
            copy.start()
    if projects:
        scaled_ref = take(0)
        held = at_chunk % slots
        sums = own_ref[...] + got_ref[...]
        mean = sums[0:1] / tokens
        scale = lax.rsqrt(sums[1:2] / tokens - mean * mean + 1e-05)
        stat_ref[0:1] = mean
        stat_ref[1:2] = scale
        scaled = (scale * basis_ref[:, at_chunk * chunk : at_chunk * chunk + chunk]).astype(BF16)
        scaled_ref[...] = scaled
        offset = jnp.sum(scaled.astype(F32) * mean, axis=1, keepdims=True)

    def gather(j):
        pltpu.make_async_copy(
            act_ref.at[pl.ds(0, ROWS), pl.ds(0, chunk)], buf_ref.at[into, pl.ds(0, ROWS)], sem.at[j]
        ).wait()

    def add_sums(j):
        at = pl.ds(pl.multiple_of(j * ROWS, ROWS), ROWS)
        for lo in range(0, chunk, LANES):
            here = slice(lo, min(lo + LANES, chunk))
            x = buf_ref[into, at, here].astype(F32)
            wide = (ROWS // 8, 8, x.shape[1])
            acc_ref[0:8, here] += jnp.sum(x.reshape(wide), axis=0)
            acc_ref[8:16, here] += jnp.sum((x * x).reshape(wide), axis=0)

    def project(j):
        at = pl.ds(pl.multiple_of(j * ROWS, ROWS), ROWS)
        part_here = lax.dot_general(
            scaled_ref[...], buf_ref[held, at, :], NT, preferred_element_type=F32
        ) - offset
        if not starts:
            part_here = part_here + part_ref[j]
        proj_ref[j] = part_here.astype(proj_ref.dtype)

    if loads is not None:
        acc_ref[...] = jnp.zeros_like(acc_ref)
    if loads is None:
        pl.loop(0, rows)(project)
    elif not projects:

        @pl.loop(0, rows)
        def _(j):
            gather(j)
            add_sums(j)

    else:
        project(0)

        @pl.loop(1, rows)
        def _(j):
            gather(j - 1)
            add_sums(j - 1)
            project(j)

        gather(rows - 1)
        add_sums(rows - 1)
    if loads is not None:
        sums_ref[0:1] = jnp.sum(acc_ref[0:8], axis=0, keepdims=True)
        sums_ref[1:2] = jnp.sum(acc_ref[8:16], axis=0, keepdims=True)


def stream(tokens, chunk, act, loads, buf, at, own, got, basis_t, part, last):
    rows, cols = act.shape[0], basis_t.shape[0]
    vmem = pl.BlockSpec(memory_space=pltpu.VMEM)
    args, in_specs, outs, scratch, aliases = [], [], [], [], {}
    if loads is not None:
        args.append(act)
        in_specs.append(pl.BlockSpec(memory_space=pl.ANY))
        outs += [pltpu.VMEM((KEEP, rows, chunk), BF16), jax.ShapeDtypeStruct((2, chunk), F32)]
        scratch += [pltpu.VMEM((16, chunk), F32), pltpu.SemaphoreType.DMA((rows // ROWS,))]
    if loads != 0:
        if loads is not None:
            aliases = {len(args): 0}
        args.append(buf)
        in_specs.append(vmem)
    if at is not None:
        args += [own, got, basis_t]
        in_specs += [vmem] * 3
        if part is not None:
            args.append(part)
            in_specs.append(vmem)
        outs += [
            jax.ShapeDtypeStruct((rows // ROWS, cols, ROWS), BF16 if last else F32),
            jax.ShapeDtypeStruct((2, chunk), F32),
        ]
        scratch.append(pltpu.VMEM((cols, chunk), BF16))
    return list(pl.pallas_call(
        functools.partial(stream_kernel, tokens, chunk, loads, at, part is None),
        in_specs=in_specs,
        out_specs=[vmem] * len(outs),
        out_shape=outs,
        scratch_shapes=scratch,
        input_output_aliases=aliases,
        compiler_params=pltpu.CompilerParams(vmem_limit_bytes=SCOPED),
        cost_estimate=pl.CostEstimate(
            flops=8 * rows * chunk * cols, bytes_accessed=2 * rows * chunk, transcendentals=0
        ),
        name="stream",
    )(*args))


def spread_kernel(blocks_ref, out_ref):
    total = jnp.sum(blocks_ref[...].astype(F32), axis=0).astype(BF16)
    for r in range(out_ref.shape[0]):
        out_ref[r] = total


def spread(blocks):
    return pl.pallas_call(
        spread_kernel,
        out_shape=jax.ShapeDtypeStruct(blocks.shape, BF16),
        compiler_params=pltpu.CompilerParams(vmem_limit_bytes=SCOPED),
        name="spread",
    )(blocks)


def cross_kernel(start, sub, proj_ref, act_ref, stats_ref, out_ref, buf_ref, sem):
    depth = buf_ref.shape[0]
    blocks = out_ref.shape[1] // sub
    copies = [
        pltpu.make_async_copy(
            act_ref.at[:, pl.ds(start + s * sub, sub)], buf_ref.at[s % depth], sem.at[s % depth]
        )
        for s in range(blocks)
    ]
    for copy in copies[:depth]:
        copy.start()
    proj = jnp.concatenate([proj_ref[r] for r in range(proj_ref.shape[0])], axis=1)
    total = jnp.sum(proj.astype(F32), axis=1, keepdims=True)
    for s, copy in enumerate(copies):
        here = slice(s * sub, s * sub + sub)
        copy.wait()
        prod = jnp.dot(proj, buf_ref[s % depth], preferred_element_type=F32)
        if s + depth < blocks:
            copies[s + depth].start()
        out_ref[:, here] = prod - total * stats_ref[0:1, here]


def cross(proj, act, stats, start):
    cols, rows = proj.shape[1], act.shape[0]
    width = stats.shape[1]
    sub = block_of(width, 512)
    vmem = pl.BlockSpec(memory_space=pltpu.VMEM)
    return pl.pallas_call(
        functools.partial(cross_kernel, start, sub),
        in_specs=[vmem, pl.BlockSpec(memory_space=pl.ANY), vmem],
        out_specs=vmem,
        out_shape=jax.ShapeDtypeStruct((cols, width), F32),
        scratch_shapes=[pltpu.VMEM((DEPTH, rows, sub), BF16), pltpu.SemaphoreType.DMA((DEPTH,))],
        compiler_params=pltpu.CompilerParams(vmem_limit_bytes=24 * MIB),
        cost_estimate=pl.CostEstimate(
            flops=8 * rows * cols * width, bytes_accessed=2 * rows * width, transcendentals=0
        ),
        name="cross",
    )(proj, act, stats)


def combine_kernel(pieces, first, last, tokens, own_ref, got_ref, stat_ref, *refs):
    i = pl.program_id(0)
    if not first:
        prev_ref, _, *refs = refs
    out_ref, gram_ref, acc_ref = refs
    cols = own_ref.shape[0]
    weighted = (own_ref[...] + got_ref[...]) * stat_ref[1:2] / tokens
    out_ref[...] = weighted
    both = jnp.concatenate(halves(weighted), axis=0)
    square = lax.dot_general(both, both, NT, preferred_element_type=F32)

    @pl.when(i == 0)
    def _():
        acc_ref[...] = square

    @pl.when(i > 0)
    def _():
        acc_ref[...] += square

    @pl.when(i == pieces - 1)
    def _():
        full = acc_ref[...]
        gram = (full[:cols, :cols] + full[cols:, cols:]) + (full[:cols, cols:] + full[cols:, :cols])
        packed = jnp.concatenate([gram[: cols // 2], gram[cols // 2 :]], axis=1)
        if not first:
            packed = packed + prev_ref[...]
        if last:
            for r in range(gram_ref.shape[0]):
                gram_ref[r] = packed
        else:
            gram_ref[...] = packed


def combine(own, got, stats, start, chunk, whole, tokens, n, prev, buffer, last):
    cols = own.shape[0]
    pieces = own.shape[1] // chunk
    first = prev is None
    here = pl.BlockSpec((cols, chunk), lambda i: (0, i))
    there = pl.BlockSpec((cols, chunk), lambda i: (0, i + start // chunk))
    packed = (n, cols // 2, 2 * cols) if last else (cols // 2, 2 * cols)
    in_specs = [here, here, pl.BlockSpec((2, chunk), lambda i: (0, i))]
    args, aliases = [own, got, stats], {}
    if not first:
        in_specs += [pl.BlockSpec((cols // 2, 2 * cols), lambda i: (0, 0)), pl.BlockSpec(memory_space=pl.ANY)]
        args += [prev, buffer]
        aliases = {4: 0}
    return pl.pallas_call(
        functools.partial(combine_kernel, pieces, first, last, tokens),
        grid=(pieces,),
        in_specs=in_specs,
        out_specs=[there, pl.BlockSpec(packed, lambda i: (0,) * len(packed))],
        out_shape=[
            jax.ShapeDtypeStruct((cols, whole), F32),
            jax.ShapeDtypeStruct(packed, F32),
        ],
        scratch_shapes=[pltpu.VMEM((2 * cols, 2 * cols), F32)],
        input_output_aliases=aliases,
        compiler_params=pltpu.CompilerParams(vmem_limit_bytes=12 * MIB),
        cost_estimate=pl.CostEstimate(
            flops=8 * cols * cols * own.shape[1], bytes_accessed=12 * cols * own.shape[1], transcendentals=0
        ),
        name="combine",
    )(*args)


def finish_kernel(gram_ref, weighted_ref, out_ref, inv_ref):
    cols = weighted_ref.shape[0]

    @pl.when(pl.program_id(0) == 0)
    def _():
        packed = jnp.sum(gram_ref[...], axis=0) / NEURONS
        gram = jnp.concatenate([packed[:, :cols], packed[:, cols:]], axis=0)
        row = lax.broadcasted_iota(jnp.int32, (cols, cols), 0)
        lane = lax.broadcasted_iota(jnp.int32, (cols, cols), 1)
        wide = jnp.concatenate([gram, (row == lane).astype(F32)], axis=1)
        tall = [wide[8 * b : 8 * b + 8] for b in range(cols // 8)]
        within = lax.broadcasted_iota(jnp.int32, (8, 1), 0)
        for k in range(cols):
            at, inner = divmod(k, 8)
            pivot_row = tall[at][inner : inner + 1]
            pivot_row = pivot_row / pivot_row[:, k : k + 1]
            for b in range(at, cols // 8):
                factor = tall[b][:, k : k + 1]
                if b == at:
                    factor = jnp.where(within > inner, factor, 0.0)
                tall[b] = tall[b] - factor * pivot_row
        wide = jnp.concatenate(tall, axis=0)
        diag = jnp.sum(jnp.where(row == lane, wide[:, :cols], 0.0), axis=1, keepdims=True)
        head, rest = halves(wide[:, cols:] * lax.rsqrt(diag))
        inv_ref[...] = jnp.concatenate([head, head, rest], axis=1)

    head, rest = halves(weighted_ref[...])
    out_ref[...] = jnp.dot(
        inv_ref[...], jnp.concatenate([head, rest, head], axis=0), preferred_element_type=F32
    )


def finish(grams, weighted):
    cols, width = weighted.shape
    nb = block_of(width, 3584)
    return pl.pallas_call(
        finish_kernel,
        grid=(width // nb,),
        in_specs=[
            pl.BlockSpec(grams.shape, lambda i: (0, 0, 0)),
            pl.BlockSpec((cols, nb), lambda i: (0, i)),
        ],
        out_specs=pl.BlockSpec((cols, nb), lambda i: (0, i)),
        out_shape=jax.ShapeDtypeStruct((cols, width), F32),
        scratch_shapes=[pltpu.VMEM((cols, 3 * cols), BF16)],
        compiler_params=pltpu.CompilerParams(vmem_limit_bytes=16 * MIB),
        name="finish",
    )(grams, weighted)


def local(activations, basis):
    tok_dev, neu_dev = activations.shape
    n, m = lax.axis_size("neuron"), lax.axis_size("token")
    tokens = tok_dev * m
    cols = basis.shape[1]
    basis_t = basis.T
    chunks = next(c for c in (CHUNKS, 7, 2, 1) if neu_dev % (128 * c) == 0)
    chunk = neu_dev // chunks

    own, got, stats = [], [], []
    part = buf = None
    for step in range(chunks + DELAY):
        loads = step if step < chunks else None
        at = step - DELAY if step >= DELAY else None
        sums = (None, None) if at is None else (own[at], got[at])
        results = stream(
            tokens, chunk, activations, loads, buf, at, *sums, basis_t, part, at == chunks - 1
        )
        if loads is not None:
            buf = results.pop(0)
            own.append(results.pop(0))
            got.append(swap_tokens(own[-1]))
        if at is not None:
            part = results.pop(0)
            stats.append(results.pop(0))

    blocks = part
    if tok_dev // n != ROWS:
        blocks = part.transpose(1, 0, 2).reshape(cols, n, tok_dev // n).transpose(1, 0, 2)
    blocks = spread(lax.all_to_all(blocks, "neuron", 0, 0))
    proj = lax.all_to_all(blocks, "neuron", 0, 0)
    if proj.shape[2] % 128:
        proj = proj.transpose(1, 0, 2).reshape(1, cols, tok_dev)

    split = chunks - max(1, chunks // 4)
    spans = [(0, split), (split, chunks)] if split else [(0, chunks)]
    stats = [jnp.concatenate(stats[lo:hi], axis=1) for lo, hi in spans]
    terms = [cross(proj, activations, stat, lo * chunk) for stat, (lo, _) in zip(stats, spans)]
    swapped = [swap_tokens(term) for term in terms]
    weighted = gram = None
    for term, got, stat, (lo, hi) in zip(terms, swapped, stats, spans):
        weighted, gram = combine(
            term, got, stat, lo * chunk, chunk, neu_dev, tokens, n, gram, weighted, hi == chunks
        )
    grams = lax.all_to_all(gram, "neuron", 0, 0)
    return finish(grams, weighted).T


def solution(mesh):
    placed = (P(("groups", "token"), "neuron"), P(("groups", "neuron"), None))
    return jax.shard_map(
        local, mesh=mesh, in_specs=placed, out_specs=P(("groups", "neuron"), None), check_vma=False
    )
```

```python
import functools

import jax
import jax.numpy as jnp
from jax import lax
from jax.experimental import pallas as pl
from jax.experimental.pallas import tpu as pltpu
from jax.sharding import PartitionSpec as P

NEURONS = 114688
F32 = jnp.float32
BF16 = jnp.bfloat16
MIB = 1 << 20
NT = (((1,), (1,)), ((), ()))
ROWS = 256
CHUNKS = 4
KEEP = 3
DEPTH = 4
SUB = 512
LANES = 512
DELAY = 2
SCOPED = 6 * MIB


def block_of(size, most):
    return max(b for b in range(128, most + 1, 128) if size % b == 0)


def swap_tokens(x):
    return lax.ppermute(x, "token", [(0, 1), (1, 0)])


def halves(x):
    head = x.astype(BF16)
    return head, (x - head.astype(F32)).astype(BF16)


def rows_at(j):
    return pl.ds(j * ROWS if isinstance(j, int) else pl.multiple_of(j * ROWS, ROWS), ROWS)


def stream_kernel(tokens, chunk, loads, at_chunk, starts, *refs):
    projects = at_chunk is not None
    refs = list(refs)
    take = refs.pop
    if loads is not None:
        act_ref = take(0)
    if loads != 0:
        buf_ref = take(0)
    if projects:
        own_ref, got_ref, basis_ref = take(0), take(0), take(0)
        if not starts:
            part_ref = take(0)
    if loads is not None:
        buf_ref, sums_ref = take(0), take(0)
    slots, tok_dev, _ = buf_ref.shape
    rows = tok_dev // ROWS
    if projects:
        proj_ref, stat_ref = take(0), take(0)
    if loads is not None:
        acc_ref, sem = take(0), take(0)
        into = loads % slots
        copies = [
            pltpu.make_async_copy(
                act_ref.at[pl.ds(j * ROWS, ROWS), pl.ds(loads * chunk, chunk)],
                buf_ref.at[into, pl.ds(j * ROWS, ROWS)],
                sem.at[j],
            )
            for j in range(rows)
        ]
        for copy in copies:
            copy.start()
    if projects:
        scaled_ref = take(0)
        held = at_chunk % slots
        sums = own_ref[...] + got_ref[...]
        mean = sums[0:1] / tokens
        scale = lax.rsqrt(sums[1:2] / tokens - mean * mean + 1e-05)
        stat_ref[0:1] = mean
        stat_ref[1:2] = scale
        scaled = (scale * basis_ref[:, at_chunk * chunk : at_chunk * chunk + chunk]).astype(BF16)
        scaled_ref[...] = scaled
        offset = jnp.sum(scaled.astype(F32) * mean, axis=1, keepdims=True)

    def gather(j):
        pltpu.make_async_copy(
            act_ref.at[pl.ds(0, ROWS), pl.ds(0, chunk)], buf_ref.at[into, pl.ds(0, ROWS)], sem.at[j]
        ).wait()

    def add_sums(j):
        at = rows_at(j)
        for lo in range(0, chunk, LANES):
            here = slice(lo, min(lo + LANES, chunk))
            x = buf_ref[into, at, here].astype(F32)
            wide = (ROWS // 8, 8, x.shape[1])
            acc_ref[0:8, here] += jnp.sum(x.reshape(wide), axis=0)
            acc_ref[8:16, here] += jnp.sum((x * x).reshape(wide), axis=0)

    def project(j):
        at = rows_at(j)
        part_here = lax.dot_general(
            scaled_ref[...], buf_ref[held, at, :], NT, preferred_element_type=F32
        ) - offset
        if not starts:
            part_here = part_here + part_ref[j]
        proj_ref[j] = part_here.astype(proj_ref.dtype)

    if loads is not None:
        acc_ref[...] = jnp.zeros_like(acc_ref)
    if loads is None:
        for j in range(rows):
            project(j)
    elif not projects:

        @pl.loop(0, rows)
        def _(j):
            gather(j)
            add_sums(j)

    else:
        project(0)

        @pl.loop(1, rows)
        def _(j):
            gather(j - 1)
            add_sums(j - 1)
            project(j)

        gather(rows - 1)
        add_sums(rows - 1)
    if loads is not None:
        sums_ref[0:1] = jnp.sum(acc_ref[0:8], axis=0, keepdims=True)
        sums_ref[1:2] = jnp.sum(acc_ref[8:16], axis=0, keepdims=True)


def stream(tokens, chunk, act, loads, buf, at, own, got, basis_t, part, last):
    rows, cols = act.shape[0], basis_t.shape[0]
    vmem = pl.BlockSpec(memory_space=pltpu.VMEM)
    args, in_specs, outs, scratch, aliases = [], [], [], [], {}
    if loads is not None:
        args.append(act)
        in_specs.append(pl.BlockSpec(memory_space=pl.ANY))
        outs += [pltpu.VMEM((KEEP, rows, chunk), BF16), jax.ShapeDtypeStruct((2, chunk), F32)]
        scratch += [pltpu.VMEM((16, chunk), F32), pltpu.SemaphoreType.DMA((rows // ROWS,))]
    if loads != 0:
        if loads is not None:
            aliases = {len(args): 0}
        args.append(buf)
        in_specs.append(vmem)
    if at is not None:
        args += [own, got, basis_t]
        in_specs += [vmem] * 3
        if part is not None:
            args.append(part)
            in_specs.append(vmem)
        outs += [
            jax.ShapeDtypeStruct((rows // ROWS, cols, ROWS), BF16 if last else F32),
            jax.ShapeDtypeStruct((2, chunk), F32),
        ]
        scratch.append(pltpu.VMEM((cols, chunk), BF16))
    return list(pl.pallas_call(
        functools.partial(stream_kernel, tokens, chunk, loads, at, part is None),
        in_specs=in_specs,
        out_specs=[vmem] * len(outs),
        out_shape=outs,
        scratch_shapes=scratch,
        input_output_aliases=aliases,
        compiler_params=pltpu.CompilerParams(vmem_limit_bytes=SCOPED),
        cost_estimate=pl.CostEstimate(
            flops=8 * rows * chunk * cols, bytes_accessed=2 * rows * chunk, transcendentals=0
        ),
        name="stream",
    )(*args))


def cross_kernel(start, sub, proj_ref, act_ref, stats_ref, out_ref, buf_ref, sem):
    depth = buf_ref.shape[0]
    blocks = out_ref.shape[1] // sub
    copies = [
        pltpu.make_async_copy(
            act_ref.at[:, pl.ds(start + s * sub, sub)], buf_ref.at[s % depth], sem.at[s % depth]
        )
        for s in range(blocks)
    ]
    for copy in copies[:depth]:
        copy.start()
    proj = jnp.concatenate([proj_ref[r] for r in range(proj_ref.shape[0])], axis=1)
    total = jnp.sum(proj.astype(F32), axis=1, keepdims=True)
    for s, copy in enumerate(copies):
        here = slice(s * sub, s * sub + sub)
        copy.wait()
        prod = jnp.dot(proj, buf_ref[s % depth], preferred_element_type=F32)
        if s + depth < blocks:
            copies[s + depth].start()
        out_ref[:, here] = prod - total * stats_ref[0:1, here]


def cross(proj, act, stats, start):
    cols, rows = proj.shape[1], act.shape[0]
    width = stats.shape[1]
    sub = block_of(width, SUB)
    vmem = pl.BlockSpec(memory_space=pltpu.VMEM)
    return pl.pallas_call(
        functools.partial(cross_kernel, start, sub),
        in_specs=[vmem, pl.BlockSpec(memory_space=pl.ANY), vmem],
        out_specs=vmem,
        out_shape=jax.ShapeDtypeStruct((cols, width), F32),
        scratch_shapes=[pltpu.VMEM((DEPTH, rows, sub), BF16), pltpu.SemaphoreType.DMA((DEPTH,))],
        compiler_params=pltpu.CompilerParams(vmem_limit_bytes=40 * MIB),
        cost_estimate=pl.CostEstimate(
            flops=8 * rows * cols * width, bytes_accessed=2 * rows * width, transcendentals=0
        ),
        name="cross",
    )(proj, act, stats)


def combine_kernel(pieces, first, last, tokens, own_ref, got_ref, stat_ref, *refs):
    i = pl.program_id(0)
    if not first:
        prev_ref, _, *refs = refs
    out_ref, gram_ref, acc_ref = refs
    cols = own_ref.shape[0]
    weighted = (own_ref[...] + got_ref[...]) * stat_ref[1:2] / tokens
    out_ref[...] = weighted
    both = jnp.concatenate(halves(weighted), axis=0)
    square = lax.dot_general(both, both, NT, preferred_element_type=F32)

    @pl.when(i == 0)
    def _():
        acc_ref[...] = square

    @pl.when(i > 0)
    def _():
        acc_ref[...] += square

    @pl.when(i == pieces - 1)
    def _():
        full = acc_ref[...]
        gram = (full[:cols, :cols] + full[cols:, cols:]) + (full[:cols, cols:] + full[cols:, :cols])
        packed = jnp.concatenate([gram[: cols // 2], gram[cols // 2 :]], axis=1)
        if not first:
            packed = packed + prev_ref[...]
        if last:
            for r in range(gram_ref.shape[0]):
                gram_ref[r] = packed
        else:
            gram_ref[...] = packed


def combine(own, got, stats, start, chunk, whole, tokens, n, prev, buffer, last):
    cols = own.shape[0]
    pieces = own.shape[1] // chunk
    first = prev is None
    here = pl.BlockSpec((cols, chunk), lambda i: (0, i))
    there = pl.BlockSpec((cols, chunk), lambda i: (0, i + start // chunk))
    packed = (n, cols // 2, 2 * cols) if last else (cols // 2, 2 * cols)
    in_specs = [here, here, pl.BlockSpec((2, chunk), lambda i: (0, i))]
    args, aliases = [own, got, stats], {}
    if not first:
        in_specs += [pl.BlockSpec((cols // 2, 2 * cols), lambda i: (0, 0)), pl.BlockSpec(memory_space=pl.ANY)]
        args += [prev, buffer]
        aliases = {4: 0}
    return pl.pallas_call(
        functools.partial(combine_kernel, pieces, first, last, tokens),
        grid=(pieces,),
        in_specs=in_specs,
        out_specs=[there, pl.BlockSpec(packed, lambda i: (0,) * len(packed))],
        out_shape=[
            jax.ShapeDtypeStruct((cols, whole), F32),
            jax.ShapeDtypeStruct(packed, F32),
        ],
        scratch_shapes=[pltpu.VMEM((2 * cols, 2 * cols), F32)],
        input_output_aliases=aliases,
        compiler_params=pltpu.CompilerParams(vmem_limit_bytes=12 * MIB),
        cost_estimate=pl.CostEstimate(
            flops=8 * cols * cols * own.shape[1], bytes_accessed=12 * cols * own.shape[1], transcendentals=0
        ),
        name="combine",
    )(*args)


def inverse_factor(gram):
    cols = gram.shape[0]
    row = lax.broadcasted_iota(jnp.int32, (cols, cols), 0)
    lane = lax.broadcasted_iota(jnp.int32, (cols, cols), 1)
    diag = jnp.where(row == lane, gram, 0.0)
    down = lax.rsqrt(jnp.sum(diag, axis=1, keepdims=True))
    along = lax.rsqrt(jnp.sum(diag, axis=0, keepdims=True))
    gram = gram * down * along
    wide = jnp.concatenate([gram, (row == lane).astype(F32)], axis=1)
    tall = [wide[8 * b : 8 * b + 8] for b in range(cols // 8)]
    tile = tall[0].shape
    within = lax.broadcasted_iota(jnp.int32, tile, 0)

    def column(x, k):
        return jnp.broadcast_to(x[:, k : k + 1], tile)

    def line(x, i):
        return jnp.broadcast_to(x[i : i + 1], tile)

    for k in range(0, cols, 2):
        at, inner = divmod(k, 8)
        first, second = line(tall[at], inner), line(tall[at], inner + 1)
        left, right = column(tall[at], k), column(tall[at], k + 1)
        a, b, c = line(left, inner), line(right, inner), line(right, inner + 1)
        over = 1.0 / (a * c - b * b)
        a, b, c = a * over, b * over, c * over
        for t in range(at, cols // 8):
            if t > at:
                left, right = column(tall[t], k), column(tall[t], k + 1)
            by_first, by_second = c * left - b * right, a * right - b * left
            if t == at:
                if inner == 6:
                    continue
                below = within > inner + 1
                by_first, by_second = jnp.where(below, by_first, 0.0), jnp.where(below, by_second, 0.0)
            tall[t] = tall[t] - (by_first * first + by_second * second)
    wide = jnp.concatenate(tall, axis=0)
    diag = jnp.sum(jnp.where(row == lane, wide[:, :cols], 0.0), axis=1, keepdims=True)
    odd = row % 2 == 1
    beside = jnp.sum(jnp.where((row == lane + 1) & odd, wide[:, :cols], 0.0), axis=1, keepdims=True)
    above = pltpu.roll(wide, 1, 0)[:, cols:]
    diag_above = pltpu.roll(jnp.broadcast_to(diag, wide.shape), 1, 0)[:, 0:1]
    ratio = jnp.where(odd[:, 0:1], beside / diag_above, 0.0)
    unit = wide[:, cols:] - ratio * above
    return unit * lax.rsqrt(diag - ratio * beside) * along


def finish_kernel(gram_ref, weighted_ref, out_ref, inv_ref):
    cols = weighted_ref.shape[0]

    @pl.when(pl.program_id(0) == 0)
    def _():
        packed = jnp.sum(gram_ref[...], axis=0) / NEURONS
        gram = jnp.concatenate([packed[:, :cols], packed[:, cols:]], axis=0)
        head, rest = halves(inverse_factor(gram))
        inv_ref[...] = jnp.concatenate([head, head, rest], axis=1)

    head, rest = halves(weighted_ref[...])
    out_ref[...] = jnp.dot(
        inv_ref[...], jnp.concatenate([head, rest, head], axis=0), preferred_element_type=F32
    )


def finish(grams, weighted):
    cols, width = weighted.shape
    nb = block_of(width, 3584)
    return pl.pallas_call(
        finish_kernel,
        grid=(width // nb,),
        in_specs=[
            pl.BlockSpec(grams.shape, lambda i: (0, 0, 0)),
            pl.BlockSpec((cols, nb), lambda i: (0, i)),
        ],
        out_specs=pl.BlockSpec((cols, nb), lambda i: (0, i)),
        out_shape=jax.ShapeDtypeStruct((cols, width), F32),
        scratch_shapes=[pltpu.VMEM((cols, 3 * cols), BF16)],
        compiler_params=pltpu.CompilerParams(vmem_limit_bytes=16 * MIB),
        name="finish",
    )(grams, weighted)


def local(activations, basis):
    tok_dev, neu_dev = activations.shape
    n, m = lax.axis_size("neuron"), lax.axis_size("token")
    tokens = tok_dev * m
    cols = basis.shape[1]
    basis_t = basis.T
    chunks = next(c for c in (CHUNKS, 7, 2, 1) if neu_dev % (128 * c) == 0)
    chunk = neu_dev // chunks

    own, got, stats = [], [], []
    part = buf = None
    for step in range(chunks + DELAY):
        loads = step if step < chunks else None
        at = step - DELAY if step >= DELAY else None
        sums = (None, None) if at is None else (own[at], got[at])
        results = stream(
            tokens, chunk, activations, loads, buf, at, *sums, basis_t, part, at == chunks - 1
        )
        if loads is not None:
            buf = results.pop(0)
            own.append(results.pop(0))
            got.append(swap_tokens(own[-1]))
        if at is not None:
            part = results.pop(0)
            stats.append(results.pop(0))

    blocks = part
    if tok_dev // n != ROWS:
        blocks = part.transpose(1, 0, 2).reshape(cols, n, tok_dev // n).transpose(1, 0, 2)
    blocks = lax.all_to_all(blocks, "neuron", 0, 0)
    block = sum(blocks[r].astype(F32) for r in range(n)).astype(BF16)
    blocks = jnp.broadcast_to(block[None], blocks.shape)
    proj = lax.all_to_all(blocks, "neuron", 0, 0)
    if proj.shape[2] % 128:
        proj = proj.transpose(1, 0, 2).reshape(1, cols, tok_dev)

    split = chunks - max(1, chunks // 4)
    spans = [(0, split), (split, chunks)] if split else [(0, chunks)]
    stats = [jnp.concatenate(stats[lo:hi], axis=1) for lo, hi in spans]
    terms = [cross(proj, activations, stat, lo * chunk) for stat, (lo, _) in zip(stats, spans)]
    swapped = [swap_tokens(term) for term in terms]
    weighted = gram = None
    for term, got, stat, (lo, hi) in zip(terms, swapped, stats, spans):
        weighted, gram = combine(
            term, got, stat, lo * chunk, chunk, neu_dev, tokens, n, gram, weighted, hi == chunks
        )
    grams = lax.all_to_all(gram, "neuron", 0, 0)
    return finish(grams, weighted).T


def solution(mesh):
    placed = (P(("groups", "token"), "neuron"), P(("groups", "neuron"), None))
    return jax.shard_map(
        local, mesh=mesh, in_specs=placed, out_specs=P(("groups", "neuron"), None), check_vma=False
    )
```

```python
import functools

import jax
import jax.numpy as jnp
from jax import lax
from jax.experimental import pallas as pl
from jax.experimental.pallas import tpu as pltpu
from jax.sharding import PartitionSpec as P

NEURONS = 114688
F32 = jnp.float32
BF16 = jnp.bfloat16
MIB = 1 << 20
NT = (((1,), (1,)), ((), ()))
ROWS = 256
CHUNKS = 4
KEEP = 3
DEPTH = 4
SUB = 512
FINAL = 2048
LANES = 512
DELAY = 2
SCOPED = 6 * MIB


def block_of(size, most):
    return max(b for b in range(128, most + 1, 128) if size % b == 0)


def swap_tokens(x):
    return lax.ppermute(x, "token", [(0, 1), (1, 0)])


def halves(x):
    head = x.astype(BF16)
    return head, (x - head.astype(F32)).astype(BF16)


def rows_at(j):
    return pl.ds(j * ROWS if isinstance(j, int) else pl.multiple_of(j * ROWS, ROWS), ROWS)


def stream_kernel(tokens, chunk, loads, at_chunk, starts, *refs):
    projects = at_chunk is not None
    refs = list(refs)
    take = refs.pop
    if loads is not None:
        act_ref = take(0)
    if loads != 0:
        buf_ref = take(0)
    if projects:
        own_ref, got_ref, basis_ref = take(0), take(0), take(0)
        if not starts:
            part_ref = take(0)
    if loads is not None:
        buf_ref, sums_ref = take(0), take(0)
    slots, tok_dev, _ = buf_ref.shape
    rows = tok_dev // ROWS
    if projects:
        proj_ref, stat_ref = take(0), take(0)
    if loads is not None:
        acc_ref, sem = take(0), take(0)
        into = loads % slots
        copies = [
            pltpu.make_async_copy(
                act_ref.at[pl.ds(j * ROWS, ROWS), pl.ds(loads * chunk, chunk)],
                buf_ref.at[into, pl.ds(j * ROWS, ROWS)],
                sem.at[j],
            )
            for j in range(rows)
        ]
        for copy in copies:
            copy.start()
    if projects:
        scaled_ref = take(0)
        held = at_chunk % slots
        sums = own_ref[...] + got_ref[...]
        mean = sums[0:1] / tokens
        scale = lax.rsqrt(sums[1:2] / tokens - mean * mean + 1e-05)
        stat_ref[0:1] = mean
        stat_ref[1:2] = scale
        scaled = (scale * basis_ref[:, at_chunk * chunk : at_chunk * chunk + chunk]).astype(BF16)
        scaled_ref[...] = scaled
        offset = jnp.sum(scaled.astype(F32) * mean, axis=1, keepdims=True)

    def gather(j):
        pltpu.make_async_copy(
            act_ref.at[pl.ds(0, ROWS), pl.ds(0, chunk)], buf_ref.at[into, pl.ds(0, ROWS)], sem.at[j]
        ).wait()

    def add_sums(j):
        at = rows_at(j)
        for lo in range(0, chunk, LANES):
            here = slice(lo, min(lo + LANES, chunk))
            x = buf_ref[into, at, here].astype(F32)
            wide = (ROWS // 8, 8, x.shape[1])
            acc_ref[0:8, here] += jnp.sum(x.reshape(wide), axis=0)
            acc_ref[8:16, here] += jnp.sum((x * x).reshape(wide), axis=0)

    def project(j):
        at = rows_at(j)
        part_here = lax.dot_general(
            scaled_ref[...], buf_ref[held, at, :], NT, preferred_element_type=F32
        ) - offset
        if not starts:
            part_here = part_here + part_ref[j]
        proj_ref[j] = part_here.astype(proj_ref.dtype)

    if loads is not None:
        acc_ref[...] = jnp.zeros_like(acc_ref)
    if loads is None:
        for j in range(rows):
            project(j)
    elif not projects:

        @pl.loop(0, rows)
        def _(j):
            gather(j)
            add_sums(j)

    else:
        project(0)

        @pl.loop(1, rows)
        def _(j):
            gather(j - 1)
            add_sums(j - 1)
            project(j)

        gather(rows - 1)
        add_sums(rows - 1)
    if loads is not None:
        sums_ref[0:1] = jnp.sum(acc_ref[0:8], axis=0, keepdims=True)
        sums_ref[1:2] = jnp.sum(acc_ref[8:16], axis=0, keepdims=True)


def stream(tokens, chunk, act, loads, buf, at, own, got, basis_t, part, last):
    rows, cols = act.shape[0], basis_t.shape[0]
    vmem = pl.BlockSpec(memory_space=pltpu.VMEM)
    args, in_specs, outs, scratch, aliases = [], [], [], [], {}
    if loads is not None:
        args.append(act)
        in_specs.append(pl.BlockSpec(memory_space=pl.ANY))
        outs += [pltpu.VMEM((KEEP, rows, chunk), BF16), jax.ShapeDtypeStruct((2, chunk), F32)]
        scratch += [pltpu.VMEM((16, chunk), F32), pltpu.SemaphoreType.DMA((rows // ROWS,))]
    if loads != 0:
        if loads is not None:
            aliases = {len(args): 0}
        args.append(buf)
        in_specs.append(vmem)
    if at is not None:
        args += [own, got, basis_t]
        in_specs += [vmem] * 3
        if part is not None:
            args.append(part)
            in_specs.append(vmem)
        outs += [
            jax.ShapeDtypeStruct((rows // ROWS, cols, ROWS), BF16 if last else F32),
            jax.ShapeDtypeStruct((2, chunk), F32),
        ]
        scratch.append(pltpu.VMEM((cols, chunk), BF16))
    return list(pl.pallas_call(
        functools.partial(stream_kernel, tokens, chunk, loads, at, part is None),
        in_specs=in_specs,
        out_specs=[vmem] * len(outs),
        out_shape=outs,
        scratch_shapes=scratch,
        input_output_aliases=aliases,
        compiler_params=pltpu.CompilerParams(vmem_limit_bytes=SCOPED),
        cost_estimate=pl.CostEstimate(
            flops=8 * rows * chunk * cols, bytes_accessed=2 * rows * chunk, transcendentals=0
        ),
        name="stream",
    )(*args))


def cross_kernel(start, sub, proj_ref, act_ref, *refs):
    *stat_refs, out_ref, buf_ref, sem = refs
    depth = buf_ref.shape[0]
    chunk = stat_refs[0].shape[1]
    blocks = out_ref.shape[1] // sub
    copies = [
        pltpu.make_async_copy(
            act_ref.at[:, pl.ds(start + s * sub, sub)], buf_ref.at[s % depth], sem.at[s % depth]
        )
        for s in range(blocks)
    ]
    for copy in copies[:depth]:
        copy.start()
    proj = jnp.concatenate([proj_ref[r] for r in range(proj_ref.shape[0])], axis=1)
    total = jnp.sum(proj.astype(F32), axis=1, keepdims=True)
    for s, copy in enumerate(copies):
        piece, at = divmod(s * sub, chunk)
        mean = stat_refs[piece][0:1, at : at + sub]
        copy.wait()
        prod = jnp.dot(proj, buf_ref[s % depth], preferred_element_type=F32)
        if s + depth < blocks:
            copies[s + depth].start()
        out_ref[:, s * sub : s * sub + sub] = prod - total * mean


def cross(proj, act, stats, start):
    cols, rows = proj.shape[1], act.shape[0]
    chunk = stats[0].shape[1]
    width = chunk * len(stats)
    sub = block_of(chunk, SUB)
    vmem = pl.BlockSpec(memory_space=pltpu.VMEM)
    return pl.pallas_call(
        functools.partial(cross_kernel, start, sub),
        in_specs=[vmem, pl.BlockSpec(memory_space=pl.ANY)] + [vmem] * len(stats),
        out_specs=vmem,
        out_shape=jax.ShapeDtypeStruct((cols, width), F32),
        scratch_shapes=[pltpu.VMEM((DEPTH, rows, sub), BF16), pltpu.SemaphoreType.DMA((DEPTH,))],
        compiler_params=pltpu.CompilerParams(vmem_limit_bytes=40 * MIB),
        cost_estimate=pl.CostEstimate(
            flops=8 * rows * cols * width, bytes_accessed=2 * rows * width, transcendentals=0
        ),
        name="cross",
    )(proj, act, *stats)


def combine_kernel(start, pieces, last, tokens, own_ref, got_ref, *refs):
    stat_refs, refs = refs[:pieces], refs[pieces:]
    if start:
        _, prev_ref, *refs = refs
    out_ref, gram_ref = refs
    cols = own_ref.shape[0]
    chunk = stat_refs[0].shape[1]
    nb = block_of(chunk, 1792)
    full = None
    for at in range(0, own_ref.shape[1], nb):
        piece, within = divmod(at, chunk)
        scale = stat_refs[piece][1:2, within : within + nb] * (1.0 / tokens)
        weighted = (own_ref[:, at : at + nb] + got_ref[:, at : at + nb]) * scale
        both = jnp.concatenate(halves(weighted), axis=0)
        out_ref[:, start + at : start + at + nb] = both
        square = lax.dot_general(both, both, NT, preferred_element_type=F32)
        full = square if full is None else full + square
    gram = (full[:cols, :cols] + full[cols:, cols:]) + (full[:cols, cols:] + full[cols:, :cols])
    packed = jnp.concatenate([gram[: cols // 2], gram[cols // 2 :]], axis=1)
    if start:
        packed = packed + prev_ref[...]
    if last:
        for r in range(gram_ref.shape[0]):
            gram_ref[r] = packed
    else:
        gram_ref[...] = packed


def combine(own, got, stats, start, whole, tokens, n, buffer, prev):
    cols, width = own.shape
    last = start + width == whole
    packed = (n, cols // 2, 2 * cols) if last else (cols // 2, 2 * cols)
    args = [own, got, *stats] + ([buffer, prev] if start else [])
    vmem = pl.BlockSpec(memory_space=pltpu.VMEM)
    return pl.pallas_call(
        functools.partial(combine_kernel, start, len(stats), last, tokens),
        in_specs=[vmem] * len(args),
        out_specs=[vmem, vmem],
        out_shape=[
            jax.ShapeDtypeStruct((2 * cols, whole), BF16),
            jax.ShapeDtypeStruct(packed, F32),
        ],
        input_output_aliases={len(args) - 2: 0} if start else {},
        compiler_params=pltpu.CompilerParams(vmem_limit_bytes=16 * MIB),
        cost_estimate=pl.CostEstimate(
            flops=8 * cols * cols * width, bytes_accessed=12 * cols * width, transcendentals=0
        ),
        name="combine",
    )(*args)


def inverse_factor(gram):
    cols = gram.shape[0]
    row = lax.broadcasted_iota(jnp.int32, (cols, cols), 0)
    lane = lax.broadcasted_iota(jnp.int32, (cols, cols), 1)
    diag = jnp.where(row == lane, gram, 0.0)
    down = lax.rsqrt(jnp.sum(diag, axis=1, keepdims=True))
    along = lax.rsqrt(jnp.sum(diag, axis=0, keepdims=True))
    gram = gram * down * along
    wide = jnp.concatenate([gram, (row == lane).astype(F32)], axis=1)
    tall = [wide[8 * b : 8 * b + 8] for b in range(cols // 8)]
    tile = tall[0].shape
    within = lax.broadcasted_iota(jnp.int32, tile, 0)

    def column(x, k):
        return jnp.broadcast_to(x[:, k : k + 1], tile)

    def line(x, i):
        return jnp.broadcast_to(x[i : i + 1], tile)

    for k in range(0, cols, 2):
        at, inner = divmod(k, 8)
        first, second = line(tall[at], inner), line(tall[at], inner + 1)
        left, right = column(tall[at], k), column(tall[at], k + 1)
        a, b, c = line(left, inner), line(right, inner), line(right, inner + 1)
        over = 1.0 / (a * c - b * b)
        a, b, c = a * over, b * over, c * over
        for t in range(at, cols // 8):
            if t > at:
                left, right = column(tall[t], k), column(tall[t], k + 1)
            by_first, by_second = c * left - b * right, a * right - b * left
            if t == at:
                if inner == 6:
                    continue
                below = within > inner + 1
                by_first, by_second = jnp.where(below, by_first, 0.0), jnp.where(below, by_second, 0.0)
            tall[t] = tall[t] - (by_first * first + by_second * second)
    wide = jnp.concatenate(tall, axis=0)
    diag = jnp.sum(jnp.where(row == lane, wide[:, :cols], 0.0), axis=1, keepdims=True)
    odd = row % 2 == 1
    beside = jnp.sum(jnp.where((row == lane + 1) & odd, wide[:, :cols], 0.0), axis=1, keepdims=True)
    above = pltpu.roll(wide, 1, 0)[:, cols:]
    diag_above = pltpu.roll(jnp.broadcast_to(diag, wide.shape), 1, 0)[:, 0:1]
    ratio = jnp.where(odd[:, 0:1], beside / diag_above, 0.0)
    unit = wide[:, cols:] - ratio * above
    return unit * lax.rsqrt(diag - ratio * beside) * along


def finish_kernel(nb, gram_ref, both_ref, out_ref, stage_ref, sem):
    cols = out_ref.shape[0]
    packed = jnp.sum(gram_ref[...], axis=0) / NEURONS
    gram = jnp.concatenate([packed[:, :cols], packed[:, cols:]], axis=0)
    head, rest = halves(inverse_factor(gram))
    twice = jnp.concatenate([head, head], axis=1)
    copies = []
    for s, at in enumerate(range(0, out_ref.shape[1], nb)):
        both = both_ref[:, at : at + nb]
        stage_ref[:, at : at + nb] = jnp.dot(twice, both, preferred_element_type=F32) + jnp.dot(
            rest, both[:cols], preferred_element_type=F32
        )
        copies.append(
            pltpu.make_async_copy(
                stage_ref.at[:, pl.ds(at, nb)], out_ref.at[:, pl.ds(at, nb)], sem.at[s]
            )
        )
        copies[-1].start()
    for copy in copies:
        copy.wait()


def finish(grams, both):
    cols, width = both.shape[0] // 2, both.shape[1]
    nb = block_of(width, FINAL)
    vmem = pl.BlockSpec(memory_space=pltpu.VMEM)
    return pl.pallas_call(
        functools.partial(finish_kernel, nb),
        in_specs=[vmem, vmem],
        out_specs=pl.BlockSpec(memory_space=pl.ANY),
        out_shape=jax.ShapeDtypeStruct((cols, width), F32),
        scratch_shapes=[pltpu.VMEM((cols, width), F32), pltpu.SemaphoreType.DMA((width // nb,))],
        compiler_params=pltpu.CompilerParams(vmem_limit_bytes=16 * MIB),
        name="finish",
    )(grams, both)


def local(activations, basis):
    tok_dev, neu_dev = activations.shape
    n, m = lax.axis_size("neuron"), lax.axis_size("token")
    tokens = tok_dev * m
    cols = basis.shape[1]
    basis_t = basis.T
    chunks = next(c for c in (CHUNKS, 7, 2, 1) if neu_dev % (128 * c) == 0)
    chunk = neu_dev // chunks

    own, got, stats = [], [], []
    part = buf = None
    for step in range(chunks + DELAY):
        loads = step if step < chunks else None
        at = step - DELAY if step >= DELAY else None
        sums = (None, None) if at is None else (own[at], got[at])
        results = stream(
            tokens, chunk, activations, loads, buf, at, *sums, basis_t, part, at == chunks - 1
        )
        if loads is not None:
            buf = results.pop(0)
            own.append(results.pop(0))
            got.append(swap_tokens(own[-1]))
        if at is not None:
            part = results.pop(0)
            stats.append(results.pop(0))

    blocks = part
    if tok_dev // n != ROWS:
        blocks = part.transpose(1, 0, 2).reshape(cols, n, tok_dev // n).transpose(1, 0, 2)
    blocks = lax.all_to_all(blocks, "neuron", 0, 0)
    block = sum(blocks[r].astype(F32) for r in range(n)).astype(BF16)
    blocks = jnp.broadcast_to(block[None], blocks.shape)
    proj = lax.all_to_all(blocks, "neuron", 0, 0)
    if proj.shape[2] % 128:
        proj = proj.transpose(1, 0, 2).reshape(1, cols, tok_dev)

    split = chunks - max(1, chunks // 4)
    spans = [(0, split), (split, chunks)] if split else [(0, chunks)]
    spans = [(lo * chunk, stats[lo:hi]) for lo, hi in spans]
    terms = [cross(proj, activations, stat, start) for start, stat in spans]
    swapped = [swap_tokens(term) for term in terms]
    both = gram = None
    for term, got, (start, stat) in zip(terms, swapped, spans):
        both, gram = combine(term, got, stat, start, neu_dev, tokens, n, both, gram)
    grams = lax.all_to_all(gram, "neuron", 0, 0)
    return finish(grams, both).T


def solution(mesh):
    placed = (P(("groups", "token"), "neuron"), P(("groups", "neuron"), None))
    return jax.shard_map(
        local, mesh=mesh, in_specs=placed, out_specs=P(("groups", "neuron"), None), check_vma=False
    )
```

```python
import functools

import jax
import jax.numpy as jnp
from jax import lax
from jax.experimental import pallas as pl
from jax.experimental.pallas import tpu as pltpu
from jax.sharding import PartitionSpec as P

NEURONS = 114688
F32 = jnp.float32
BF16 = jnp.bfloat16
MIB = 1 << 20
NT = (((1,), (1,)), ((), ()))
ROWS = 256
CHUNKS = 4
KEEP = 2
DEPTH = 4
SUB = 896
FINAL = 2048
LANES = 512
DELAY = 1
SCOPED = 6 * MIB


def block_of(size, most):
    return max(b for b in range(128, most + 1, 128) if size % b == 0)


def swap_tokens(x):
    return lax.ppermute(x, "token", [(0, 1), (1, 0)])


def halves(x):
    head = x.astype(BF16)
    return head, (x - head.astype(F32)).astype(BF16)


def rows_at(j):
    return pl.ds(j * ROWS if isinstance(j, int) else pl.multiple_of(j * ROWS, ROWS), ROWS)


def stream_kernel(tokens, chunk, loads, at_chunk, starts, ahead, *refs):
    projects = at_chunk is not None
    refs = list(refs)
    take = refs.pop
    if loads is not None or ahead:
        act_ref = take(0)
    if loads != 0:
        buf_ref = take(0)
    if projects:
        own_ref, got_ref, basis_ref = take(0), take(0), take(0)
        if not starts:
            part_ref = take(0)
    if loads is not None:
        buf_ref, sums_ref = take(0), take(0)
    slots, tok_dev, _ = buf_ref.shape
    rows = tok_dev // ROWS
    if projects:
        proj_ref, stat_ref = take(0), take(0)
    if ahead:
        ahead_ref = take(0)
    if loads is not None:
        acc_ref, sem = take(0), take(0)
        into = loads % slots
        copies = [
            pltpu.make_async_copy(
                act_ref.at[pl.ds(j * ROWS, ROWS), pl.ds(loads * chunk, chunk)],
                buf_ref.at[into, pl.ds(j * ROWS, ROWS)],
                sem.at[j],
            )
            for j in range(rows)
        ]
        for copy in copies:
            copy.start()
    if projects:
        scaled_ref = take(0)
        if ahead:
            early = pltpu.make_async_copy(act_ref.at[:, pl.ds(0, ahead)], ahead_ref, take(0))
            early.start()
        held = at_chunk % slots
        sums = own_ref[...] + got_ref[...]
        mean = sums[0:1] / tokens
        scale = lax.rsqrt(sums[1:2] / tokens - mean * mean + 1e-05)
        stat_ref[0:1] = mean
        stat_ref[1:2] = scale
        scaled = (scale * basis_ref[:, at_chunk * chunk : at_chunk * chunk + chunk]).astype(BF16)
        scaled_ref[...] = scaled
        offset = jnp.sum(scaled.astype(F32) * mean, axis=1, keepdims=True)

    def gather(j):
        pltpu.make_async_copy(
            act_ref.at[pl.ds(0, ROWS), pl.ds(0, chunk)], buf_ref.at[into, pl.ds(0, ROWS)], sem.at[j]
        ).wait()

    def add_sums(j):
        at = rows_at(j)
        for lo in range(0, chunk, LANES):
            here = slice(lo, min(lo + LANES, chunk))
            x = buf_ref[into, at, here].astype(F32)
            wide = (ROWS // 8, 8, x.shape[1])
            acc_ref[0:8, here] += jnp.sum(x.reshape(wide), axis=0)
            acc_ref[8:16, here] += jnp.sum((x * x).reshape(wide), axis=0)

    def project(j):
        at = rows_at(j)
        part_here = lax.dot_general(
            scaled_ref[...], buf_ref[held, at, :], NT, preferred_element_type=F32
        ) - offset
        if not starts:
            part_here = part_here + part_ref[j]
        proj_ref[j] = part_here.astype(proj_ref.dtype)

    if loads is not None:
        acc_ref[...] = jnp.zeros_like(acc_ref)
    if loads is None:
        for j in range(rows):
            project(j)
    elif not projects:

        @pl.loop(0, rows)
        def _(j):
            gather(j)
            add_sums(j)

    else:
        project(0)

        @pl.loop(1, rows)
        def _(j):
            gather(j - 1)
            add_sums(j - 1)
            project(j)

        gather(rows - 1)
        add_sums(rows - 1)
    if ahead:
        early.wait()
    if loads is not None:
        sums_ref[0:1] = jnp.sum(acc_ref[0:8], axis=0, keepdims=True)
        sums_ref[1:2] = jnp.sum(acc_ref[8:16], axis=0, keepdims=True)


def stream(tokens, chunk, act, loads, buf, at, own, got, basis_t, part, last, ahead):
    rows, cols = act.shape[0], basis_t.shape[0]
    vmem = pl.BlockSpec(memory_space=pltpu.VMEM)
    args, in_specs, outs, scratch, aliases = [], [], [], [], {}
    if loads is not None or ahead:
        args.append(act)
        in_specs.append(pl.BlockSpec(memory_space=pl.ANY))
    if loads is not None:
        outs += [pltpu.VMEM((KEEP, rows, chunk), BF16), jax.ShapeDtypeStruct((2, chunk), F32)]
        scratch += [pltpu.VMEM((16, chunk), F32), pltpu.SemaphoreType.DMA((rows // ROWS,))]
    if loads != 0:
        if loads is not None:
            aliases = {len(args): 0}
        args.append(buf)
        in_specs.append(vmem)
    if at is not None:
        args += [own, got, basis_t]
        in_specs += [vmem] * 3
        if part is not None:
            args.append(part)
            in_specs.append(vmem)
        outs += [
            jax.ShapeDtypeStruct((rows // ROWS, cols, ROWS), BF16 if last else F32),
            jax.ShapeDtypeStruct((2, chunk), F32),
        ]
        scratch.append(pltpu.VMEM((cols, chunk), BF16))
    if ahead:
        outs.append(pltpu.VMEM((rows, ahead), BF16))
        scratch.append(pltpu.SemaphoreType.DMA)
    return list(pl.pallas_call(
        functools.partial(stream_kernel, tokens, chunk, loads, at, part is None, ahead),
        in_specs=in_specs,
        out_specs=[vmem] * len(outs),
        out_shape=outs,
        scratch_shapes=scratch,
        input_output_aliases=aliases,
        compiler_params=pltpu.CompilerParams(vmem_limit_bytes=SCOPED),
        cost_estimate=pl.CostEstimate(
            flops=8 * rows * chunk * cols, bytes_accessed=2 * rows * chunk, transcendentals=0
        ),
        name="stream",
    )(*args))


def cross_kernel(start, last, proj_ref, act_ref, ahead_ref, *refs):
    if last:
        *stat_refs, out_ref, buf_ref, sem = refs
    else:
        *stat_refs, out_ref, next_ref, buf_ref, sem, next_sem = refs
    depth, _, sub = buf_ref.shape
    chunk = stat_refs[0].shape[1]
    blocks = out_ref.shape[1] // sub
    copies = [
        pltpu.make_async_copy(
            act_ref.at[:, pl.ds(start + s * sub, sub)], buf_ref.at[s % depth], sem.at[s % depth]
        )
        for s in range(1, blocks)
    ]
    if not last:
        copies.append(
            pltpu.make_async_copy(act_ref.at[:, pl.ds(start + blocks * sub, sub)], next_ref, next_sem)
        )
    for copy in copies[:depth]:
        copy.start()
    proj = jnp.concatenate([proj_ref[r] for r in range(proj_ref.shape[0])], axis=1)
    total = jnp.sum(proj.astype(F32), axis=1, keepdims=True)
    for s in range(blocks):
        piece, at = divmod(s * sub, chunk)
        mean = stat_refs[piece][0:1, at : at + sub]
        if s:
            copies[s - 1].wait()
        act = buf_ref[s % depth] if s else ahead_ref[...]
        prod = jnp.dot(proj, act, preferred_element_type=F32)
        if s and s - 1 + depth < len(copies):
            copies[s - 1 + depth].start()
        out_ref[:, s * sub : s * sub + sub] = prod - total * mean
    if not last:
        copies[-1].wait()


def cross(proj, act, ahead, stats, start):
    cols, rows = proj.shape[1], act.shape[0]
    sub = ahead.shape[1]
    width = stats[0].shape[1] * len(stats)
    last = start + width == act.shape[1]
    vmem = pl.BlockSpec(memory_space=pltpu.VMEM)
    outs = [jax.ShapeDtypeStruct((cols, width), F32)]
    scratch = [pltpu.VMEM((DEPTH, rows, sub), BF16), pltpu.SemaphoreType.DMA((DEPTH,))]
    if not last:
        outs.append(pltpu.VMEM((rows, sub), BF16))
        scratch.append(pltpu.SemaphoreType.DMA)
    return pl.pallas_call(
        functools.partial(cross_kernel, start, last),
        in_specs=[vmem, pl.BlockSpec(memory_space=pl.ANY), vmem] + [vmem] * len(stats),
        out_specs=[vmem] * len(outs),
        out_shape=outs,
        scratch_shapes=scratch,
        compiler_params=pltpu.CompilerParams(vmem_limit_bytes=40 * MIB),
        cost_estimate=pl.CostEstimate(
            flops=8 * rows * cols * width, bytes_accessed=2 * rows * width, transcendentals=0
        ),
        name="cross",
    )(proj, act, ahead, *stats)


def combine_kernel(start, pieces, last, tokens, own_ref, got_ref, *refs):
    stat_refs, refs = refs[:pieces], refs[pieces:]
    if start:
        _, prev_ref, *refs = refs
    out_ref, gram_ref = refs
    cols = own_ref.shape[0]
    chunk = stat_refs[0].shape[1]
    nb = block_of(chunk, 1792)
    full = None
    for at in range(0, own_ref.shape[1], nb):
        piece, within = divmod(at, chunk)
        scale = stat_refs[piece][1:2, within : within + nb] * (1.0 / tokens)
        weighted = (own_ref[:, at : at + nb] + got_ref[:, at : at + nb]) * scale
        both = jnp.concatenate(halves(weighted), axis=0)
        out_ref[:, start + at : start + at + nb] = both
        square = lax.dot_general(both, both, NT, preferred_element_type=F32)
        full = square if full is None else full + square
    gram = (full[:cols, :cols] + full[cols:, cols:]) + (full[:cols, cols:] + full[cols:, :cols])
    packed = jnp.concatenate([gram[: cols // 2], gram[cols // 2 :]], axis=1)
    if start:
        packed = packed + prev_ref[...]
    if last:
        for r in range(gram_ref.shape[0]):
            gram_ref[r] = packed
    else:
        gram_ref[...] = packed


def combine(own, got, stats, start, whole, tokens, n, buffer, prev):
    cols, width = own.shape
    last = start + width == whole
    packed = (n, cols // 2, 2 * cols) if last else (cols // 2, 2 * cols)
    args = [own, got, *stats] + ([buffer, prev] if start else [])
    vmem = pl.BlockSpec(memory_space=pltpu.VMEM)
    return pl.pallas_call(
        functools.partial(combine_kernel, start, len(stats), last, tokens),
        in_specs=[vmem] * len(args),
        out_specs=[vmem, vmem],
        out_shape=[
            jax.ShapeDtypeStruct((2 * cols, whole), BF16),
            jax.ShapeDtypeStruct(packed, F32),
        ],
        input_output_aliases={len(args) - 2: 0} if start else {},
        compiler_params=pltpu.CompilerParams(vmem_limit_bytes=16 * MIB),
        cost_estimate=pl.CostEstimate(
            flops=8 * cols * cols * width, bytes_accessed=12 * cols * width, transcendentals=0
        ),
        name="combine",
    )(*args)


def inverse_factor(gram):
    cols = gram.shape[0]
    row = lax.broadcasted_iota(jnp.int32, (cols, cols), 0)
    lane = lax.broadcasted_iota(jnp.int32, (cols, cols), 1)
    diag = jnp.where(row == lane, gram, 0.0)
    down = lax.rsqrt(jnp.sum(diag, axis=1, keepdims=True))
    along = lax.rsqrt(jnp.sum(diag, axis=0, keepdims=True))
    gram = gram * down * along
    wide = jnp.concatenate([gram, (row == lane).astype(F32)], axis=1)
    tall = [wide[8 * b : 8 * b + 8] for b in range(cols // 8)]
    tile = tall[0].shape
    within = lax.broadcasted_iota(jnp.int32, tile, 0)

    def column(x, k):
        return jnp.broadcast_to(x[:, k : k + 1], tile)

    def line(x, i):
        return jnp.broadcast_to(x[i : i + 1], tile)

    for k in range(0, cols, 2):
        at, inner = divmod(k, 8)
        first, second = line(tall[at], inner), line(tall[at], inner + 1)
        left, right = column(tall[at], k), column(tall[at], k + 1)
        a, b, c = line(left, inner), line(right, inner), line(right, inner + 1)
        over = 1.0 / (a * c - b * b)
        a, b, c = a * over, b * over, c * over
        for t in range(at, cols // 8):
            if t > at:
                left, right = column(tall[t], k), column(tall[t], k + 1)
            by_first, by_second = c * left - b * right, a * right - b * left
            if t == at:
                if inner == 6:
                    continue
                below = within > inner + 1
                by_first, by_second = jnp.where(below, by_first, 0.0), jnp.where(below, by_second, 0.0)
            tall[t] = tall[t] - (by_first * first + by_second * second)
    wide = jnp.concatenate(tall, axis=0)
    diag = jnp.sum(jnp.where(row == lane, wide[:, :cols], 0.0), axis=1, keepdims=True)
    odd = row % 2 == 1
    beside = jnp.sum(jnp.where((row == lane + 1) & odd, wide[:, :cols], 0.0), axis=1, keepdims=True)
    above = pltpu.roll(wide, 1, 0)[:, cols:]
    diag_above = pltpu.roll(jnp.broadcast_to(diag, wide.shape), 1, 0)[:, 0:1]
    ratio = jnp.where(odd[:, 0:1], beside / diag_above, 0.0)
    unit = wide[:, cols:] - ratio * above
    return unit * lax.rsqrt(diag - ratio * beside) * along


def finish_kernel(nb, gram_ref, both_ref, out_ref, stage_ref, sem):
    cols = out_ref.shape[0]
    packed = jnp.sum(gram_ref[...], axis=0) / NEURONS
    gram = jnp.concatenate([packed[:, :cols], packed[:, cols:]], axis=0)
    head, rest = halves(inverse_factor(gram))
    twice = jnp.concatenate([head, head], axis=1)
    copies = []
    for s, at in enumerate(range(0, out_ref.shape[1], nb)):
        both = both_ref[:, at : at + nb]
        stage_ref[:, at : at + nb] = jnp.dot(twice, both, preferred_element_type=F32) + jnp.dot(
            rest, both[:cols], preferred_element_type=F32
        )
        copies.append(
            pltpu.make_async_copy(
                stage_ref.at[:, pl.ds(at, nb)], out_ref.at[:, pl.ds(at, nb)], sem.at[s]
            )
        )
        copies[-1].start()
    for copy in copies:
        copy.wait()


def finish(grams, both):
    cols, width = both.shape[0] // 2, both.shape[1]
    nb = block_of(width, FINAL)
    vmem = pl.BlockSpec(memory_space=pltpu.VMEM)
    return pl.pallas_call(
        functools.partial(finish_kernel, nb),
        in_specs=[vmem, vmem],
        out_specs=pl.BlockSpec(memory_space=pl.ANY),
        out_shape=jax.ShapeDtypeStruct((cols, width), F32),
        scratch_shapes=[pltpu.VMEM((cols, width), F32), pltpu.SemaphoreType.DMA((width // nb,))],
        compiler_params=pltpu.CompilerParams(vmem_limit_bytes=16 * MIB),
        name="finish",
    )(grams, both)


def local(activations, basis):
    tok_dev, neu_dev = activations.shape
    n, m = lax.axis_size("neuron"), lax.axis_size("token")
    tokens = tok_dev * m
    cols = basis.shape[1]
    basis_t = basis.T
    chunks = next(c for c in (CHUNKS, 7, 2, 1) if neu_dev % (128 * c) == 0)
    chunk = neu_dev // chunks

    own, got, stats = [], [], []
    part = buf = None
    for step in range(chunks + DELAY):
        loads = step if step < chunks else None
        at = step - DELAY if step >= DELAY else None
        sums = (None, None) if at is None else (own[at], got[at])
        results = stream(
            tokens, chunk, activations, loads, buf, at, *sums, basis_t, part,
            at == chunks - 1, block_of(chunk, SUB) if at == chunks - 1 else 0,
        )
        if loads is not None:
            buf = results.pop(0)
            own.append(results.pop(0))
            got.append(swap_tokens(own[-1]))
        if at is not None:
            part = results.pop(0)
            stats.append(results.pop(0))
    (ahead,) = results

    blocks = part
    if tok_dev // n != ROWS:
        blocks = part.transpose(1, 0, 2).reshape(cols, n, tok_dev // n).transpose(1, 0, 2)
    blocks = lax.all_to_all(blocks, "neuron", 0, 0)
    block = sum(blocks[r].astype(F32) for r in range(n)).astype(BF16)
    blocks = jnp.broadcast_to(block[None], blocks.shape)
    proj = lax.all_to_all(blocks, "neuron", 0, 0)
    if proj.shape[2] % 128:
        proj = proj.transpose(1, 0, 2).reshape(1, cols, tok_dev)

    split = chunks - max(1, chunks // 4)
    spans = [(0, split), (split, chunks)] if split else [(0, chunks)]
    spans = [(lo * chunk, stats[lo:hi]) for lo, hi in spans]
    terms, swapped = [], []
    for start, stat in spans:
        term, *rest = cross(proj, activations, ahead, stat, start)
        ahead = rest[0] if rest else None
        terms.append(term)
        swapped.append(swap_tokens(term))
    both = gram = None
    for term, got, (start, stat) in zip(terms, swapped, spans):
        both, gram = combine(term, got, stat, start, neu_dev, tokens, n, both, gram)
    grams = lax.all_to_all(gram, "neuron", 0, 0)
    return finish(grams, both).T


def solution(mesh):
    placed = (P(("groups", "token"), "neuron"), P(("groups", "neuron"), None))
    return jax.shard_map(
        local, mesh=mesh, in_specs=placed, out_specs=P(("groups", "neuron"), None), check_vma=False
    )
```

```python
import functools

import jax
import jax.numpy as jnp
from jax import lax
from jax.experimental import pallas as pl
from jax.experimental.pallas import tpu as pltpu
from jax.sharding import PartitionSpec as P

NEURONS = 114688
F32 = jnp.float32
BF16 = jnp.bfloat16
MIB = 1 << 20
NT = (((1,), (1,)), ((), ()))
ROWS = 256
CHUNKS = 4
KEEP = 3
PEEK = 3
DEPTH = 4
SUB = 896
FINAL = 2048
LANES = 512
DELAY = 2
SCOPED = 3 * MIB


def block_of(size, most):
    return max(b for b in range(128, most + 1, 128) if size % b == 0)


def swap_tokens(x):
    return lax.ppermute(x, "token", [(0, 1), (1, 0)])


def halves(x):
    head = x.astype(BF16)
    return head, (x - head.astype(F32)).astype(BF16)


def rows_at(j):
    return pl.ds(j * ROWS if isinstance(j, int) else pl.multiple_of(j * ROWS, ROWS), ROWS)


def stream_kernel(tokens, chunk, loads, at_chunk, starts, ahead, given, peek, *refs):
    projects = at_chunk is not None
    refs = list(refs)
    take = refs.pop
    if loads is not None or ahead:
        act_ref = take(0)
    if loads != 0:
        buf_ref = take(0)
    if projects:
        own_ref, got_ref, basis_ref = take(0), take(0), take(0)
        if not starts:
            part_ref = take(0)
    if loads is not None:
        buf_ref, sums_ref = take(0), take(0)
    slots, tok_dev, _ = buf_ref.shape
    rows = tok_dev // ROWS
    if projects:
        proj_ref, stat_ref = take(0), take(0)
    if ahead:
        ahead_ref = take(0)
    if loads is not None:
        acc_ref, sem = take(0), take(0)
        into = loads % slots
        copies = [
            pltpu.make_async_copy(
                act_ref.at[pl.ds(j * ROWS, ROWS), pl.ds(origin * chunk, chunk)],
                buf_ref.at[origin % slots, pl.ds(j * ROWS, ROWS)],
                sem.at[j + (rows if origin > loads else 0)],
            )
            for origin, lo, hi in ((loads, given, rows), (loads + 1, 0, peek))
            for j in range(lo, hi)
        ]
        for copy in copies:
            copy.start()
    if projects:
        scaled_ref = take(0)
        if ahead:
            early = pltpu.make_async_copy(act_ref.at[:, pl.ds(0, ahead)], ahead_ref, take(0))
            early.start()
        held = at_chunk % slots
        sums = own_ref[...] + got_ref[...]
        mean = sums[0:1] / tokens
        scale = lax.rsqrt(sums[1:2] / tokens - mean * mean + 1e-05)
        stat_ref[0:1] = mean
        stat_ref[1:2] = scale
        scaled = (scale * basis_ref[:, at_chunk * chunk : at_chunk * chunk + chunk]).astype(BF16)
        scaled_ref[...] = scaled
        offset = jnp.sum(scaled.astype(F32) * mean, axis=1, keepdims=True)

    def gather(j):
        pltpu.make_async_copy(
            act_ref.at[pl.ds(0, ROWS), pl.ds(0, chunk)], buf_ref.at[into, pl.ds(0, ROWS)], sem.at[j]
        ).wait()

    def add_sums(j):
        at = rows_at(j)
        for lo in range(0, chunk, LANES):
            here = slice(lo, min(lo + LANES, chunk))
            x = buf_ref[into, at, here].astype(F32)
            wide = (ROWS // 8, 8, x.shape[1])
            acc_ref[0:8, here] += jnp.sum(x.reshape(wide), axis=0)
            acc_ref[8:16, here] += jnp.sum((x * x).reshape(wide), axis=0)

    def project(j):
        at = rows_at(j)
        part_here = lax.dot_general(
            scaled_ref[...], buf_ref[held, at, :], NT, preferred_element_type=F32
        ) - offset
        if not starts:
            part_here = part_here + part_ref[j]
        proj_ref[j] = part_here.astype(proj_ref.dtype)

    if loads is not None:
        acc_ref[...] = jnp.zeros_like(acc_ref)
    if loads is None:
        for j in range(rows):
            project(j)
    elif not projects:
        for j in range(given):
            add_sums(j)

        @pl.loop(given, rows)
        def _(j):
            gather(j)
            add_sums(j)

        for copy in copies[rows - given :]:
            copy.wait()

    else:
        project(0)

        @pl.loop(1, rows)
        def _(j):
            gather(j - 1)
            add_sums(j - 1)
            project(j)

        gather(rows - 1)
        add_sums(rows - 1)
    if ahead:
        early.wait()
    if loads is not None:
        sums_ref[0:1] = jnp.sum(acc_ref[0:8], axis=0, keepdims=True)
        sums_ref[1:2] = jnp.sum(acc_ref[8:16], axis=0, keepdims=True)


def stream(tokens, chunk, act, loads, buf, at, own, got, basis_t, part, last, ahead, given, peek):
    rows, cols = act.shape[0], basis_t.shape[0]
    vmem = pl.BlockSpec(memory_space=pltpu.VMEM)
    args, in_specs, outs, scratch, aliases = [], [], [], [], {}
    if loads is not None or ahead:
        args.append(act)
        in_specs.append(pl.BlockSpec(memory_space=pl.ANY))
    if loads is not None:
        outs += [pltpu.VMEM((KEEP, rows, chunk), BF16), jax.ShapeDtypeStruct((2, chunk), F32)]
        scratch += [pltpu.VMEM((16, chunk), F32), pltpu.SemaphoreType.DMA((rows // ROWS + peek,))]
    if loads != 0:
        if loads is not None:
            aliases = {len(args): 0}
        args.append(buf)
        in_specs.append(vmem)
    if at is not None:
        args += [own, got, basis_t]
        in_specs += [vmem] * 3
        if part is not None:
            args.append(part)
            in_specs.append(vmem)
        outs += [
            jax.ShapeDtypeStruct((rows // ROWS, cols, ROWS), BF16 if last else F32),
            jax.ShapeDtypeStruct((2, chunk), F32),
        ]
        scratch.append(pltpu.VMEM((cols, chunk), BF16))
    if ahead:
        outs.append(pltpu.VMEM((rows, ahead), BF16))
        scratch.append(pltpu.SemaphoreType.DMA)
    return list(pl.pallas_call(
        functools.partial(stream_kernel, tokens, chunk, loads, at, part is None, ahead, given, peek),
        in_specs=in_specs,
        out_specs=[vmem] * len(outs),
        out_shape=outs,
        scratch_shapes=scratch,
        input_output_aliases=aliases,
        compiler_params=pltpu.CompilerParams(vmem_limit_bytes=SCOPED),
        cost_estimate=pl.CostEstimate(
            flops=8 * rows * chunk * cols, bytes_accessed=2 * rows * chunk, transcendentals=0
        ),
        name="stream",
    )(*args))


def cross_kernel(start, last, proj_ref, act_ref, ahead_ref, *refs):
    if last:
        *stat_refs, out_ref, buf_ref, sem = refs
    else:
        *stat_refs, out_ref, next_ref, buf_ref, sem, next_sem = refs
    depth, _, sub = buf_ref.shape
    chunk = stat_refs[0].shape[1]
    blocks = out_ref.shape[1] // sub
    copies = [
        pltpu.make_async_copy(
            act_ref.at[:, pl.ds(start + s * sub, sub)], buf_ref.at[s % depth], sem.at[s % depth]
        )
        for s in range(1, blocks)
    ]
    if not last:
        copies.append(
            pltpu.make_async_copy(act_ref.at[:, pl.ds(start + blocks * sub, sub)], next_ref, next_sem)
        )
    for copy in copies[:depth]:
        copy.start()
    proj = jnp.concatenate([proj_ref[r] for r in range(proj_ref.shape[0])], axis=1)
    total = jnp.sum(proj.astype(F32), axis=1, keepdims=True)
    for s in range(blocks):
        piece, at = divmod(s * sub, chunk)
        mean = stat_refs[piece][0:1, at : at + sub]
        if s:
            copies[s - 1].wait()
        act = buf_ref[s % depth] if s else ahead_ref[...]
        prod = jnp.dot(proj, act, preferred_element_type=F32)
        if s and s - 1 + depth < len(copies):
            copies[s - 1 + depth].start()
        out_ref[:, s * sub : s * sub + sub] = prod - total * mean
    if not last:
        copies[-1].wait()


def cross(proj, act, ahead, stats, start):
    cols, rows = proj.shape[1], act.shape[0]
    sub = ahead.shape[1]
    width = stats[0].shape[1] * len(stats)
    last = start + width == act.shape[1]
    vmem = pl.BlockSpec(memory_space=pltpu.VMEM)
    outs = [jax.ShapeDtypeStruct((cols, width), F32)]
    scratch = [pltpu.VMEM((DEPTH, rows, sub), BF16), pltpu.SemaphoreType.DMA((DEPTH,))]
    if not last:
        outs.append(pltpu.VMEM((rows, sub), BF16))
        scratch.append(pltpu.SemaphoreType.DMA)
    return pl.pallas_call(
        functools.partial(cross_kernel, start, last),
        in_specs=[vmem, pl.BlockSpec(memory_space=pl.ANY), vmem] + [vmem] * len(stats),
        out_specs=[vmem] * len(outs),
        out_shape=outs,
        scratch_shapes=scratch,
        compiler_params=pltpu.CompilerParams(vmem_limit_bytes=40 * MIB),
        cost_estimate=pl.CostEstimate(
            flops=8 * rows * cols * width, bytes_accessed=2 * rows * width, transcendentals=0
        ),
        name="cross",
    )(proj, act, ahead, *stats)


def combine_kernel(start, pieces, last, tokens, own_ref, got_ref, *refs):
    stat_refs, refs = refs[:pieces], refs[pieces:]
    if start:
        _, prev_ref, *refs = refs
    out_ref, gram_ref = refs
    cols = own_ref.shape[0]
    chunk = stat_refs[0].shape[1]
    nb = block_of(chunk, 1792)
    full = None
    for at in range(0, own_ref.shape[1], nb):
        piece, within = divmod(at, chunk)
        scale = stat_refs[piece][1:2, within : within + nb] * (1.0 / tokens)
        weighted = (own_ref[:, at : at + nb] + got_ref[:, at : at + nb]) * scale
        both = jnp.concatenate(halves(weighted), axis=0)
        out_ref[:, start + at : start + at + nb] = both
        square = lax.dot_general(both, both, NT, preferred_element_type=F32)
        full = square if full is None else full + square
    gram = (full[:cols, :cols] + full[cols:, cols:]) + (full[:cols, cols:] + full[cols:, :cols])
    packed = jnp.concatenate([gram[: cols // 2], gram[cols // 2 :]], axis=1)
    if start:
        packed = packed + prev_ref[...]
    if last:
        for r in range(gram_ref.shape[0]):
            gram_ref[r] = packed
    else:
        gram_ref[...] = packed


def combine(own, got, stats, start, whole, tokens, n, buffer, prev):
    cols, width = own.shape
    last = start + width == whole
    packed = (n, cols // 2, 2 * cols) if last else (cols // 2, 2 * cols)
    args = [own, got, *stats] + ([buffer, prev] if start else [])
    vmem = pl.BlockSpec(memory_space=pltpu.VMEM)
    return pl.pallas_call(
        functools.partial(combine_kernel, start, len(stats), last, tokens),
        in_specs=[vmem] * len(args),
        out_specs=[vmem, vmem],
        out_shape=[
            jax.ShapeDtypeStruct((2 * cols, whole), BF16),
            jax.ShapeDtypeStruct(packed, F32),
        ],
        input_output_aliases={len(args) - 2: 0} if start else {},
        compiler_params=pltpu.CompilerParams(vmem_limit_bytes=16 * MIB),
        cost_estimate=pl.CostEstimate(
            flops=8 * cols * cols * width, bytes_accessed=12 * cols * width, transcendentals=0
        ),
        name="combine",
    )(*args)


def inverse_factor(gram):
    cols = gram.shape[0]
    row = lax.broadcasted_iota(jnp.int32, (cols, cols), 0)
    lane = lax.broadcasted_iota(jnp.int32, (cols, cols), 1)
    diag = jnp.where(row == lane, gram, 0.0)
    down = lax.rsqrt(jnp.sum(diag, axis=1, keepdims=True))
    along = lax.rsqrt(jnp.sum(diag, axis=0, keepdims=True))
    gram = gram * down * along
    wide = jnp.concatenate([gram, (row == lane).astype(F32)], axis=1)
    tall = [wide[8 * b : 8 * b + 8] for b in range(cols // 8)]
    tile = tall[0].shape
    within = lax.broadcasted_iota(jnp.int32, tile, 0)

    def column(x, k):
        return jnp.broadcast_to(x[:, k : k + 1], tile)

    def line(x, i):
        return jnp.broadcast_to(x[i : i + 1], tile)

    def factors_of(a, b, c):
        over = 1.0 / (a * c - b * b)
        a, b, c = a * over, b * over, c * over
        return lambda x, y: (c * x - b * y, a * y - b * x)

    for at in range(cols // 8):
        base = 8 * at
        rows = [line(tall[at], j) for j in range(8)]
        below = range(at, cols // 8)
        columns = {t: [column(tall[t], base + j) for j in range(8)] for t in below}
        pivots = {(i, j): line(columns[at][j], i) for i in range(8) for j in range(i + 1)}
        change = {t: 0.0 for t in below}
        for z in range(0, 8, 2):
            factors = factors_of(pivots[z, z], pivots[z + 1, z], pivots[z + 1, z + 1])
            later = range(z + 2, 8)
            for t in below:
                first, second = factors(columns[t][z], columns[t][z + 1])
                for j in later:
                    columns[t][j] = columns[t][j] - (first * pivots[j, z] + second * pivots[j, z + 1])
                if t == at:
                    first = jnp.where(within > z + 1, first, 0.0)
                    second = jnp.where(within > z + 1, second, 0.0)
                change[t] = change[t] + (first * rows[z] + second * rows[z + 1])
            own = {i: factors(pivots[i, z], pivots[i, z + 1]) for i in later}
            for i in later:
                first, second = own[i]
                for j in range(z + 2, i + 1):
                    pivots[i, j] = pivots[i, j] - (first * pivots[j, z] + second * pivots[j, z + 1])
                rows[i] = rows[i] - (first * rows[z] + second * rows[z + 1])
        for t in below:
            tall[t] = tall[t] - change[t]
    wide = jnp.concatenate(tall, axis=0)
    diag = jnp.sum(jnp.where(row == lane, wide[:, :cols], 0.0), axis=1, keepdims=True)
    odd = row % 2 == 1
    beside = jnp.sum(jnp.where((row == lane + 1) & odd, wide[:, :cols], 0.0), axis=1, keepdims=True)
    above = pltpu.roll(wide, 1, 0)[:, cols:]
    diag_above = pltpu.roll(jnp.broadcast_to(diag, wide.shape), 1, 0)[:, 0:1]
    ratio = jnp.where(odd[:, 0:1], beside / diag_above, 0.0)
    unit = wide[:, cols:] - ratio * above
    return unit * lax.rsqrt(diag - ratio * beside) * along


def finish_kernel(nb, gram_ref, both_ref, out_ref, stage_ref, sem):
    cols = out_ref.shape[0]
    packed = jnp.sum(gram_ref[...], axis=0) / NEURONS
    gram = jnp.concatenate([packed[:, :cols], packed[:, cols:]], axis=0)
    head, rest = halves(inverse_factor(gram))
    twice = jnp.concatenate([head, head], axis=1)
    copies = []
    for s, at in enumerate(range(0, out_ref.shape[1], nb)):
        both = both_ref[:, at : at + nb]
        stage_ref[:, at : at + nb] = jnp.dot(twice, both, preferred_element_type=F32) + jnp.dot(
            rest, both[:cols], preferred_element_type=F32
        )
        copies.append(
            pltpu.make_async_copy(
                stage_ref.at[:, pl.ds(at, nb)], out_ref.at[:, pl.ds(at, nb)], sem.at[s]
            )
        )
        copies[-1].start()
    for copy in copies:
        copy.wait()


def finish(grams, both):
    cols, width = both.shape[0] // 2, both.shape[1]
    nb = block_of(width, FINAL)
    vmem = pl.BlockSpec(memory_space=pltpu.VMEM)
    return pl.pallas_call(
        functools.partial(finish_kernel, nb),
        in_specs=[vmem, vmem],
        out_specs=pl.BlockSpec(memory_space=pl.ANY),
        out_shape=jax.ShapeDtypeStruct((cols, width), F32),
        scratch_shapes=[pltpu.VMEM((cols, width), F32), pltpu.SemaphoreType.DMA((width // nb,))],
        compiler_params=pltpu.CompilerParams(vmem_limit_bytes=16 * MIB),
        name="finish",
    )(grams, both)


def local(activations, basis):
    tok_dev, neu_dev = activations.shape
    n, m = lax.axis_size("neuron"), lax.axis_size("token")
    tokens = tok_dev * m
    cols = basis.shape[1]
    basis_t = basis.T
    chunks = next(c for c in (CHUNKS, 7, 2, 1) if neu_dev % (128 * c) == 0)
    chunk = neu_dev // chunks

    own, got, stats = [], [], []
    part = buf = None
    peek = PEEK if DELAY > 1 and chunks > 1 else 0
    for step in range(chunks + DELAY):
        loads = step if step < chunks else None
        at = step - DELAY if step >= DELAY else None
        sums = (None, None) if at is None else (own[at], got[at])
        results = stream(
            tokens, chunk, activations, loads, buf, at, *sums, basis_t, part,
            at == chunks - 1, block_of(chunk, SUB) if at == chunks - 1 else 0,
            peek if step == 1 else 0, peek if step == 0 else 0,
        )
        if loads is not None:
            buf = results.pop(0)
            own.append(results.pop(0))
            got.append(swap_tokens(own[-1]))
        if at is not None:
            part = results.pop(0)
            stats.append(results.pop(0))
    (ahead,) = results

    blocks = part
    if tok_dev // n != ROWS:
        blocks = part.transpose(1, 0, 2).reshape(cols, n, tok_dev // n).transpose(1, 0, 2)
    blocks = lax.all_to_all(blocks, "neuron", 0, 0)
    block = sum(blocks[r].astype(F32) for r in range(n)).astype(BF16)
    blocks = jnp.broadcast_to(block[None], blocks.shape)
    proj = lax.all_to_all(blocks, "neuron", 0, 0)
    if proj.shape[2] % 128:
        proj = proj.transpose(1, 0, 2).reshape(1, cols, tok_dev)

    split = chunks - max(1, chunks // 4)
    spans = [(0, split), (split, chunks)] if split else [(0, chunks)]
    spans = [(lo * chunk, stats[lo:hi]) for lo, hi in spans]
    terms, swapped = [], []
    for start, stat in spans:
        term, *rest = cross(proj, activations, ahead, stat, start)
        ahead = rest[0] if rest else None
        terms.append(term)
        swapped.append(swap_tokens(term))
    both = gram = None
    for term, got, (start, stat) in zip(terms, swapped, spans):
        both, gram = combine(term, got, stat, start, neu_dev, tokens, n, both, gram)
    grams = lax.all_to_all(gram, "neuron", 0, 0)
    return finish(grams, both).T


def solution(mesh):
    placed = (P(("groups", "token"), "neuron"), P(("groups", "neuron"), None))
    return jax.shard_map(
        local, mesh=mesh, in_specs=placed, out_specs=P(("groups", "neuron"), None), check_vma=False
    )
```

```python
import functools

import jax
import jax.numpy as jnp
from jax import lax
from jax.experimental import pallas as pl
from jax.experimental.pallas import tpu as pltpu
from jax.sharding import PartitionSpec as P

NEURONS = 114688
F32 = jnp.float32
BF16 = jnp.bfloat16
MIB = 1 << 20
NT = (((1,), (1,)), ((), ()))
ROWS = 256
CHUNKS = 4
KEEP = 3
PEEK = 3
TURN = 1
DEPTH = 4
SUB = 896
FINAL = 2048
LANES = 512
DELAY = 2
SCOPED = 3 * MIB


def block_of(size, most):
    return max(b for b in range(128, most + 1, 128) if size % b == 0)


def swap_tokens(x):
    return lax.ppermute(x, "token", [(0, 1), (1, 0)])


def halves(x):
    head = x.astype(BF16)
    return head, (x - head.astype(F32)).astype(BF16)


def rows_at(j):
    return pl.ds(j * ROWS if isinstance(j, int) else pl.multiple_of(j * ROWS, ROWS), ROWS)


def turned(origin, chunk):
    return origin < TURN and chunk % ROWS == 0


def stream_kernel(tokens, chunk, loads, at_chunk, starts, ahead, given, peek, *refs):
    projects = at_chunk is not None
    refs = list(refs)
    take = refs.pop
    if loads is not None or ahead:
        act_ref = take(0)
    if loads != 0:
        buf_ref = take(0)
    if projects:
        own_ref, got_ref, basis_ref = take(0), take(0), take(0)
        if not starts:
            part_ref = take(0)
    if loads is not None:
        buf_ref, sums_ref = take(0), take(0)
    slots, tok_dev, _ = buf_ref.shape
    rows = tok_dev // ROWS
    if projects:
        proj_ref, stat_ref = take(0), take(0)
    if ahead:
        ahead_ref = take(0)
    if loads is not None:
        acc_ref, sem = take(0), take(0)
        into = loads % slots
        copies = [
            pltpu.make_async_copy(
                act_ref.at[pl.ds(j * ROWS, ROWS), pl.ds(origin * chunk, chunk)],
                buf_ref.at[origin % slots, pl.ds(j * ROWS, ROWS)],
                sem.at[j + (rows if origin > loads else 0)],
            )
            for origin, lo, hi in ((loads, given, rows), (loads + 1, 0, peek))
            for j in range(lo, hi)
        ]
        for copy in copies:
            copy.start()
    if projects:
        scaled_ref = take(0)
        if ahead:
            early = pltpu.make_async_copy(act_ref.at[:, pl.ds(0, ahead)], ahead_ref, take(0))
            early.start()
        held = at_chunk % slots
        sums = own_ref[...] + got_ref[...]
        mean = sums[0:1] / tokens
        scale = lax.rsqrt(sums[1:2] / tokens - mean * mean + 1e-05)
        stat_ref[0:1] = mean
        stat_ref[1:2] = scale
        scaled = (scale * basis_ref[:, at_chunk * chunk : at_chunk * chunk + chunk]).astype(BF16)
        scaled_ref[...] = scaled
        offset = jnp.sum(scaled.astype(F32) * mean, axis=1, keepdims=True)

    def gather(j):
        pltpu.make_async_copy(
            act_ref.at[pl.ds(0, ROWS), pl.ds(0, chunk)], buf_ref.at[into, pl.ds(0, ROWS)], sem.at[j]
        ).wait()

    def add_sums(j):
        at = rows_at(j)
        for lo in range(0, chunk, LANES):
            here = slice(lo, min(lo + LANES, chunk))
            x = buf_ref[into, at, here].astype(F32)
            wide = (ROWS // 8, 8, x.shape[1])
            acc_ref[0:8, here] += jnp.sum(x.reshape(wide), axis=0)
            acc_ref[8:16, here] += jnp.sum((x * x).reshape(wide), axis=0)

    def turn(j):
        at = rows_at(j)
        for lo in range(0, chunk, ROWS):
            buf_ref[into, at, lo : lo + ROWS] = buf_ref[into, at, lo : lo + ROWS].T

    def project(j):
        at = rows_at(j)
        if turned(at_chunk, chunk):
            part_here = -offset
            for lo in range(0, chunk, ROWS):
                part_here = part_here + jnp.dot(
                    scaled_ref[:, lo : lo + ROWS],
                    buf_ref[held, at, lo : lo + ROWS],
                    preferred_element_type=F32,
                )
        else:
            part_here = lax.dot_general(
                scaled_ref[...], buf_ref[held, at, :], NT, preferred_element_type=F32
            ) - offset
        if not starts:
            part_here = part_here + part_ref[j]
        proj_ref[j] = part_here.astype(proj_ref.dtype)

    if loads is not None:
        acc_ref[...] = jnp.zeros_like(acc_ref)
    if loads is None:
        for j in range(rows):
            project(j)
    elif not projects:
        for j in range(given):
            add_sums(j)
            if turned(loads, chunk):
                turn(j)

        @pl.loop(given, rows)
        def _(j):
            gather(j)
            add_sums(j)
            if turned(loads, chunk):
                turn(j)

        for copy in copies[rows - given :]:
            copy.wait()

    else:
        project(0)

        @pl.loop(1, rows)
        def _(j):
            gather(j - 1)
            add_sums(j - 1)
            project(j)

        gather(rows - 1)
        add_sums(rows - 1)
    if ahead:
        early.wait()
    if loads is not None:
        sums_ref[0:1] = jnp.sum(acc_ref[0:8], axis=0, keepdims=True)
        sums_ref[1:2] = jnp.sum(acc_ref[8:16], axis=0, keepdims=True)


def stream(tokens, chunk, act, loads, buf, at, own, got, basis_t, part, last, ahead, given, peek):
    rows, cols = act.shape[0], basis_t.shape[0]
    vmem = pl.BlockSpec(memory_space=pltpu.VMEM)
    args, in_specs, outs, scratch, aliases = [], [], [], [], {}
    if loads is not None or ahead:
        args.append(act)
        in_specs.append(pl.BlockSpec(memory_space=pl.ANY))
    if loads is not None:
        outs += [pltpu.VMEM((KEEP, rows, chunk), BF16), jax.ShapeDtypeStruct((2, chunk), F32)]
        scratch += [pltpu.VMEM((16, chunk), F32), pltpu.SemaphoreType.DMA((rows // ROWS + peek,))]
    if loads != 0:
        if loads is not None:
            aliases = {len(args): 0}
        args.append(buf)
        in_specs.append(vmem)
    if at is not None:
        args += [own, got, basis_t]
        in_specs += [vmem] * 3
        if part is not None:
            args.append(part)
            in_specs.append(vmem)
        outs += [
            jax.ShapeDtypeStruct((rows // ROWS, cols, ROWS), BF16 if last else F32),
            jax.ShapeDtypeStruct((2, chunk), F32),
        ]
        scratch.append(pltpu.VMEM((cols, chunk), BF16))
    if ahead:
        outs.append(pltpu.VMEM((rows, ahead), BF16))
        scratch.append(pltpu.SemaphoreType.DMA)
    return list(pl.pallas_call(
        functools.partial(stream_kernel, tokens, chunk, loads, at, part is None, ahead, given, peek),
        in_specs=in_specs,
        out_specs=[vmem] * len(outs),
        out_shape=outs,
        scratch_shapes=scratch,
        input_output_aliases=aliases,
        compiler_params=pltpu.CompilerParams(vmem_limit_bytes=SCOPED),
        cost_estimate=pl.CostEstimate(
            flops=8 * rows * chunk * cols, bytes_accessed=2 * rows * chunk, transcendentals=0
        ),
        name="stream",
    )(*args))


def cross_kernel(start, last, proj_ref, act_ref, ahead_ref, *refs):
    if last:
        *stat_refs, out_ref, buf_ref, sem = refs
    else:
        *stat_refs, out_ref, next_ref, buf_ref, sem, next_sem = refs
    depth, _, sub = buf_ref.shape
    chunk = stat_refs[0].shape[1]
    blocks = out_ref.shape[1] // sub
    copies = [
        pltpu.make_async_copy(
            act_ref.at[:, pl.ds(start + s * sub, sub)], buf_ref.at[s % depth], sem.at[s % depth]
        )
        for s in range(1, blocks)
    ]
    if not last:
        copies.append(
            pltpu.make_async_copy(act_ref.at[:, pl.ds(start + blocks * sub, sub)], next_ref, next_sem)
        )
    for copy in copies[:depth]:
        copy.start()
    proj = jnp.concatenate([proj_ref[r] for r in range(proj_ref.shape[0])], axis=1)
    total = jnp.sum(proj.astype(F32), axis=1, keepdims=True)
    for s in range(blocks):
        piece, at = divmod(s * sub, chunk)
        mean = stat_refs[piece][0:1, at : at + sub]
        if s:
            copies[s - 1].wait()
        act = buf_ref[s % depth] if s else ahead_ref[...]
        prod = jnp.dot(proj, act, preferred_element_type=F32)
        if s and s - 1 + depth < len(copies):
            copies[s - 1 + depth].start()
        out_ref[:, s * sub : s * sub + sub] = prod - total * mean
    if not last:
        copies[-1].wait()


def cross(proj, act, ahead, stats, start):
    cols, rows = proj.shape[1], act.shape[0]
    sub = ahead.shape[1]
    width = stats[0].shape[1] * len(stats)
    last = start + width == act.shape[1]
    vmem = pl.BlockSpec(memory_space=pltpu.VMEM)
    outs = [jax.ShapeDtypeStruct((cols, width), F32)]
    scratch = [pltpu.VMEM((DEPTH, rows, sub), BF16), pltpu.SemaphoreType.DMA((DEPTH,))]
    if not last:
        outs.append(pltpu.VMEM((rows, sub), BF16))
        scratch.append(pltpu.SemaphoreType.DMA)
    return pl.pallas_call(
        functools.partial(cross_kernel, start, last),
        in_specs=[vmem, pl.BlockSpec(memory_space=pl.ANY), vmem] + [vmem] * len(stats),
        out_specs=[vmem] * len(outs),
        out_shape=outs,
        scratch_shapes=scratch,
        compiler_params=pltpu.CompilerParams(vmem_limit_bytes=40 * MIB),
        cost_estimate=pl.CostEstimate(
            flops=8 * rows * cols * width, bytes_accessed=2 * rows * width, transcendentals=0
        ),
        name="cross",
    )(proj, act, ahead, *stats)


def combine_kernel(start, pieces, last, tokens, own_ref, got_ref, *refs):
    stat_refs, refs = refs[:pieces], refs[pieces:]
    if start:
        _, prev_ref, *refs = refs
    out_ref, gram_ref = refs
    cols = own_ref.shape[0]
    chunk = stat_refs[0].shape[1]
    nb = block_of(chunk, 1792)
    full = None
    for at in range(0, own_ref.shape[1], nb):
        piece, within = divmod(at, chunk)
        scale = stat_refs[piece][1:2, within : within + nb] * (1.0 / tokens)
        weighted = (own_ref[:, at : at + nb] + got_ref[:, at : at + nb]) * scale
        both = jnp.concatenate(halves(weighted), axis=0)
        out_ref[:, start + at : start + at + nb] = both
        square = lax.dot_general(both, both, NT, preferred_element_type=F32)
        full = square if full is None else full + square
    gram = (full[:cols, :cols] + full[cols:, cols:]) + (full[:cols, cols:] + full[cols:, :cols])
    packed = jnp.concatenate([gram[: cols // 2], gram[cols // 2 :]], axis=1)
    if start:
        packed = packed + prev_ref[...]
    if last:
        for r in range(gram_ref.shape[0]):
            gram_ref[r] = packed
    else:
        gram_ref[...] = packed


def combine(own, got, stats, start, whole, tokens, n, buffer, prev):
    cols, width = own.shape
    last = start + width == whole
    packed = (n, cols // 2, 2 * cols) if last else (cols // 2, 2 * cols)
    args = [own, got, *stats] + ([buffer, prev] if start else [])
    vmem = pl.BlockSpec(memory_space=pltpu.VMEM)
    return pl.pallas_call(
        functools.partial(combine_kernel, start, len(stats), last, tokens),
        in_specs=[vmem] * len(args),
        out_specs=[vmem, vmem],
        out_shape=[
            jax.ShapeDtypeStruct((2 * cols, whole), BF16),
            jax.ShapeDtypeStruct(packed, F32),
        ],
        input_output_aliases={len(args) - 2: 0} if start else {},
        compiler_params=pltpu.CompilerParams(vmem_limit_bytes=16 * MIB),
        cost_estimate=pl.CostEstimate(
            flops=8 * cols * cols * width, bytes_accessed=12 * cols * width, transcendentals=0
        ),
        name="combine",
    )(*args)


def inverse_factor(gram):
    cols = gram.shape[0]
    row = lax.broadcasted_iota(jnp.int32, (cols, cols), 0)
    lane = lax.broadcasted_iota(jnp.int32, (cols, cols), 1)
    diag = jnp.where(row == lane, gram, 0.0)
    down = lax.rsqrt(jnp.sum(diag, axis=1, keepdims=True))
    along = lax.rsqrt(jnp.sum(diag, axis=0, keepdims=True))
    gram = gram * down * along
    wide = jnp.concatenate([gram, (row == lane).astype(F32)], axis=1)
    tall = [wide[8 * b : 8 * b + 8] for b in range(cols // 8)]
    tile = tall[0].shape
    within = lax.broadcasted_iota(jnp.int32, tile, 0)

    def column(x, k):
        return jnp.broadcast_to(x[:, k : k + 1], tile)

    def line(x, i):
        return jnp.broadcast_to(x[i : i + 1], tile)

    def factors_of(a, b, c):
        over = 1.0 / (a * c - b * b)
        a, b, c = a * over, b * over, c * over
        return lambda x, y: (c * x - b * y, a * y - b * x)

    for at in range(cols // 8):
        base = 8 * at
        rows = [line(tall[at], j) for j in range(8)]
        below = range(at, cols // 8)
        columns = {t: [column(tall[t], base + j) for j in range(8)] for t in below}
        pivots = {(i, j): line(columns[at][j], i) for i in range(8) for j in range(i + 1)}
        change = {t: 0.0 for t in below}
        for z in range(0, 8, 2):
            factors = factors_of(pivots[z, z], pivots[z + 1, z], pivots[z + 1, z + 1])
            later = range(z + 2, 8)
            for t in below:
                first, second = factors(columns[t][z], columns[t][z + 1])
                for j in later:
                    columns[t][j] = columns[t][j] - (first * pivots[j, z] + second * pivots[j, z + 1])
                if t == at:
                    first = jnp.where(within > z + 1, first, 0.0)
                    second = jnp.where(within > z + 1, second, 0.0)
                change[t] = change[t] + (first * rows[z] + second * rows[z + 1])
            own = {i: factors(pivots[i, z], pivots[i, z + 1]) for i in later}
            for i in later:
                first, second = own[i]
                for j in range(z + 2, i + 1):
                    pivots[i, j] = pivots[i, j] - (first * pivots[j, z] + second * pivots[j, z + 1])
                rows[i] = rows[i] - (first * rows[z] + second * rows[z + 1])
        for t in below:
            tall[t] = tall[t] - change[t]
    wide = jnp.concatenate(tall, axis=0)
    diag = jnp.sum(jnp.where(row == lane, wide[:, :cols], 0.0), axis=1, keepdims=True)
    odd = row % 2 == 1
    beside = jnp.sum(jnp.where((row == lane + 1) & odd, wide[:, :cols], 0.0), axis=1, keepdims=True)
    above = pltpu.roll(wide, 1, 0)[:, cols:]
    diag_above = pltpu.roll(jnp.broadcast_to(diag, wide.shape), 1, 0)[:, 0:1]
    ratio = jnp.where(odd[:, 0:1], beside / diag_above, 0.0)
    unit = wide[:, cols:] - ratio * above
    return unit * lax.rsqrt(diag - ratio * beside) * along


def finish_kernel(nb, gram_ref, both_ref, out_ref, stage_ref, sem):
    cols = out_ref.shape[0]
    packed = jnp.sum(gram_ref[...], axis=0) / NEURONS
    gram = jnp.concatenate([packed[:, :cols], packed[:, cols:]], axis=0)
    head, rest = halves(inverse_factor(gram))
    twice = jnp.concatenate([head, head], axis=1)
    copies = []
    for s, at in enumerate(range(0, out_ref.shape[1], nb)):
        both = both_ref[:, at : at + nb]
        stage_ref[:, at : at + nb] = jnp.dot(twice, both, preferred_element_type=F32) + jnp.dot(
            rest, both[:cols], preferred_element_type=F32
        )
        copies.append(
            pltpu.make_async_copy(
                stage_ref.at[:, pl.ds(at, nb)], out_ref.at[:, pl.ds(at, nb)], sem.at[s]
            )
        )
        copies[-1].start()
    for copy in copies:
        copy.wait()


def finish(grams, both):
    cols, width = both.shape[0] // 2, both.shape[1]
    nb = block_of(width, FINAL)
    vmem = pl.BlockSpec(memory_space=pltpu.VMEM)
    return pl.pallas_call(
        functools.partial(finish_kernel, nb),
        in_specs=[vmem, vmem],
        out_specs=pl.BlockSpec(memory_space=pl.ANY),
        out_shape=jax.ShapeDtypeStruct((cols, width), F32),
        scratch_shapes=[pltpu.VMEM((cols, width), F32), pltpu.SemaphoreType.DMA((width // nb,))],
        compiler_params=pltpu.CompilerParams(vmem_limit_bytes=16 * MIB),
        name="finish",
    )(grams, both)


def local(activations, basis):
    tok_dev, neu_dev = activations.shape
    n, m = lax.axis_size("neuron"), lax.axis_size("token")
    tokens = tok_dev * m
    cols = basis.shape[1]
    basis_t = basis.T
    chunks = next(c for c in (CHUNKS, 7, 2, 1) if neu_dev % (128 * c) == 0)
    chunk = neu_dev // chunks

    own, got, stats = [], [], []
    part = buf = None
    peek = PEEK if DELAY > 1 and chunks > 1 else 0
    for step in range(chunks + DELAY):
        loads = step if step < chunks else None
        at = step - DELAY if step >= DELAY else None
        sums = (None, None) if at is None else (own[at], got[at])
        results = stream(
            tokens, chunk, activations, loads, buf, at, *sums, basis_t, part,
            at == chunks - 1, block_of(chunk, SUB) if at == chunks - 1 else 0,
            peek if step == 1 else 0, peek if step == 0 else 0,
        )
        if loads is not None:
            buf = results.pop(0)
            own.append(results.pop(0))
            got.append(swap_tokens(own[-1]))
        if at is not None:
            part = results.pop(0)
            stats.append(results.pop(0))
    (ahead,) = results

    blocks = part
    if tok_dev // n != ROWS:
        blocks = part.transpose(1, 0, 2).reshape(cols, n, tok_dev // n).transpose(1, 0, 2)
    blocks = lax.all_to_all(blocks, "neuron", 0, 0)
    block = sum(blocks[r].astype(F32) for r in range(n)).astype(BF16)
    blocks = jnp.broadcast_to(block[None], blocks.shape)
    proj = lax.all_to_all(blocks, "neuron", 0, 0)
    if proj.shape[2] % 128:
        proj = proj.transpose(1, 0, 2).reshape(1, cols, tok_dev)

    split = chunks - max(1, chunks // 4)
    spans = [(0, split), (split, chunks)] if split else [(0, chunks)]
    spans = [(lo * chunk, stats[lo:hi]) for lo, hi in spans]
    terms, swapped = [], []
    for start, stat in spans:
        term, *rest = cross(proj, activations, ahead, stat, start)
        ahead = rest[0] if rest else None
        terms.append(term)
        swapped.append(swap_tokens(term))
    both = gram = None
    for term, got, (start, stat) in zip(terms, swapped, spans):
        both, gram = combine(term, got, stat, start, neu_dev, tokens, n, both, gram)
    grams = lax.all_to_all(gram, "neuron", 0, 0)
    return finish(grams, both).T


def solution(mesh):
    placed = (P(("groups", "token"), "neuron"), P(("groups", "neuron"), None))
    return jax.shard_map(
        local, mesh=mesh, in_specs=placed, out_specs=P(("groups", "neuron"), None), check_vma=False
    )
```

```python
import functools

import jax
import jax.numpy as jnp
from jax import lax
from jax.experimental import pallas as pl
from jax.experimental.pallas import tpu as pltpu
from jax.sharding import PartitionSpec as P

NEURONS = 114688
F32 = jnp.float32
BF16 = jnp.bfloat16
MIB = 1 << 20
NT = (((1,), (1,)), ((), ()))
ROWS = 256
CHUNKS = 4
KEEP = 3
PEEK = 4
TURN = 1
DEPTH = 3
SUB = 896
FINAL = 2048
LANES = 512
DELAY = 2
SCOPED = 3 * MIB


def block_of(size, most):
    return max(b for b in range(128, most + 1, 128) if size % b == 0)


def swap_tokens(x):
    return lax.ppermute(x, "token", [(0, 1), (1, 0)])


def halves(x):
    head = x.astype(BF16)
    return head, (x - head.astype(F32)).astype(BF16)


def rows_at(j):
    return pl.ds(j * ROWS if isinstance(j, int) else pl.multiple_of(j * ROWS, ROWS), ROWS)


def turned(origin, chunk):
    return origin < TURN and chunk % ROWS == 0


def stream_kernel(tokens, chunk, loads, at_chunk, starts, ahead, given, peek, *refs):
    projects = at_chunk is not None
    refs = list(refs)
    take = refs.pop
    if loads is not None or ahead:
        act_ref = take(0)
    if loads != 0:
        buf_ref = take(0)
    if projects:
        own_ref, got_ref, basis_ref = take(0), take(0), take(0)
        if not starts:
            part_ref = take(0)
    if loads is not None:
        buf_ref, sums_ref = take(0), take(0)
    slots, tok_dev, _ = buf_ref.shape
    rows = tok_dev // ROWS
    if projects:
        proj_ref, stat_ref = take(0), take(0)
    if ahead:
        ahead_ref = take(0)
    if loads is not None:
        acc_ref, sem = take(0), take(0)
        into = loads % slots
        copies = [
            pltpu.make_async_copy(
                act_ref.at[pl.ds(j * ROWS, ROWS), pl.ds(origin * chunk, chunk)],
                buf_ref.at[origin % slots, pl.ds(j * ROWS, ROWS)],
                sem.at[j + (rows if origin > loads else 0)],
            )
            for origin, lo, hi in ((loads, given, rows), (loads + 1, 0, peek))
            for j in range(lo, hi)
        ]
        for copy in copies:
            copy.start()
    if projects:
        scaled_ref = take(0)
        if ahead:
            early = pltpu.make_async_copy(act_ref.at[:, pl.ds(0, ahead)], ahead_ref, take(0))
            early.start()
        held = at_chunk % slots
        sums = own_ref[...] + got_ref[...]
        mean = sums[0:1] / tokens
        scale = lax.rsqrt(sums[1:2] / tokens - mean * mean + 1e-05)
        stat_ref[0:1] = mean
        stat_ref[1:2] = scale
        scaled = (scale * basis_ref[:, at_chunk * chunk : at_chunk * chunk + chunk]).astype(BF16)
        scaled_ref[...] = scaled
        offset = jnp.sum(scaled.astype(F32) * mean, axis=1, keepdims=True)

    def gather(j):
        pltpu.make_async_copy(
            act_ref.at[pl.ds(0, ROWS), pl.ds(0, chunk)], buf_ref.at[into, pl.ds(0, ROWS)], sem.at[j]
        ).wait()

    def add_sums(j):
        at = rows_at(j)
        for lo in range(0, chunk, LANES):
            here = slice(lo, min(lo + LANES, chunk))
            x = buf_ref[into, at, here].astype(F32)
            wide = (ROWS // 8, 8, x.shape[1])
            acc_ref[0:8, here] += jnp.sum(x.reshape(wide), axis=0)
            acc_ref[8:16, here] += jnp.sum((x * x).reshape(wide), axis=0)

    def turn(j):
        at = rows_at(j)
        for lo in range(0, chunk, ROWS):
            buf_ref[into, at, lo : lo + ROWS] = buf_ref[into, at, lo : lo + ROWS].T

    def project(j):
        at = rows_at(j)
        if turned(at_chunk, chunk):
            part_here = -offset
            for lo in range(0, chunk, ROWS):
                part_here = part_here + jnp.dot(
                    scaled_ref[:, lo : lo + ROWS],
                    buf_ref[held, at, lo : lo + ROWS],
                    preferred_element_type=F32,
                )
        else:
            part_here = lax.dot_general(
                scaled_ref[...], buf_ref[held, at, :], NT, preferred_element_type=F32
            ) - offset
        if not starts:
            part_here = part_here + part_ref[j]
        proj_ref[j] = part_here.astype(proj_ref.dtype)

    if loads is not None:
        acc_ref[...] = jnp.zeros_like(acc_ref)
    if loads is None:
        for j in range(rows):
            project(j)
    elif not projects:
        for j in range(given):
            add_sums(j)
            if turned(loads, chunk):
                turn(j)

        @pl.loop(given, rows)
        def _(j):
            gather(j)
            add_sums(j)
            if turned(loads, chunk):
                turn(j)

        for copy in copies[rows - given :]:
            copy.wait()

    else:
        project(0)

        @pl.loop(1, rows)
        def _(j):
            gather(j - 1)
            add_sums(j - 1)
            project(j)

        gather(rows - 1)
        add_sums(rows - 1)
    if ahead:
        early.wait()
    if loads is not None:
        sums_ref[0:1] = jnp.sum(acc_ref[0:8], axis=0, keepdims=True)
        sums_ref[1:2] = jnp.sum(acc_ref[8:16], axis=0, keepdims=True)


def stream(tokens, chunk, act, loads, buf, at, own, got, basis_t, part, last, ahead, given, peek):
    rows, cols = act.shape[0], basis_t.shape[0]
    vmem = pl.BlockSpec(memory_space=pltpu.VMEM)
    args, in_specs, outs, scratch, aliases = [], [], [], [], {}
    if loads is not None or ahead:
        args.append(act)
        in_specs.append(pl.BlockSpec(memory_space=pl.ANY))
    if loads is not None:
        outs += [pltpu.VMEM((KEEP, rows, chunk), BF16), jax.ShapeDtypeStruct((2, chunk), F32)]
        scratch += [pltpu.VMEM((16, chunk), F32), pltpu.SemaphoreType.DMA((rows // ROWS + peek,))]
    if loads != 0:
        if loads is not None:
            aliases = {len(args): 0}
        args.append(buf)
        in_specs.append(vmem)
    if at is not None:
        args += [own, got, basis_t]
        in_specs += [vmem] * 3
        if part is not None:
            args.append(part)
            in_specs.append(vmem)
        outs += [
            jax.ShapeDtypeStruct((rows // ROWS, cols, ROWS), BF16 if last else F32),
            jax.ShapeDtypeStruct((2, chunk), F32),
        ]
        scratch.append(pltpu.VMEM((cols, chunk), BF16))
    if ahead:
        outs.append(pltpu.VMEM((rows, ahead), BF16))
        scratch.append(pltpu.SemaphoreType.DMA)
    return list(pl.pallas_call(
        functools.partial(stream_kernel, tokens, chunk, loads, at, part is None, ahead, given, peek),
        in_specs=in_specs,
        out_specs=[vmem] * len(outs),
        out_shape=outs,
        scratch_shapes=scratch,
        input_output_aliases=aliases,
        compiler_params=pltpu.CompilerParams(vmem_limit_bytes=SCOPED),
        cost_estimate=pl.CostEstimate(
            flops=8 * rows * chunk * cols, bytes_accessed=2 * rows * chunk, transcendentals=0
        ),
        name="stream",
    )(*args))


def cross_kernel(start, last, proj_ref, act_ref, ahead_ref, *refs):
    if last:
        *stat_refs, out_ref, buf_ref, sem = refs
    else:
        *stat_refs, out_ref, next_ref, buf_ref, sem, next_sem = refs
    depth, _, sub = buf_ref.shape
    chunk = stat_refs[0].shape[1]
    blocks = out_ref.shape[1] // sub
    copies = [
        pltpu.make_async_copy(
            act_ref.at[:, pl.ds(start + s * sub, sub)], buf_ref.at[s % depth], sem.at[s % depth]
        )
        for s in range(1, blocks)
    ]
    if not last:
        copies.append(
            pltpu.make_async_copy(act_ref.at[:, pl.ds(start + blocks * sub, sub)], next_ref, next_sem)
        )
    for copy in copies[:depth]:
        copy.start()
    proj = jnp.concatenate([proj_ref[r] for r in range(proj_ref.shape[0])], axis=1)
    total = jnp.sum(proj.astype(F32), axis=1, keepdims=True)
    for s in range(blocks):
        piece, at = divmod(s * sub, chunk)
        mean = stat_refs[piece][0:1, at : at + sub]
        if s:
            copies[s - 1].wait()
        act = buf_ref[s % depth] if s else ahead_ref[...]
        prod = jnp.dot(proj, act, preferred_element_type=F32)
        if s and s - 1 + depth < len(copies):
            copies[s - 1 + depth].start()
        out_ref[:, s * sub : s * sub + sub] = prod - total * mean
    if not last:
        copies[-1].wait()


def cross(proj, act, ahead, stats, start):
    cols, rows = proj.shape[1], act.shape[0]
    sub = ahead.shape[1]
    width = stats[0].shape[1] * len(stats)
    last = start + width == act.shape[1]
    vmem = pl.BlockSpec(memory_space=pltpu.VMEM)
    outs = [jax.ShapeDtypeStruct((cols, width), F32)]
    scratch = [pltpu.VMEM((DEPTH, rows, sub), BF16), pltpu.SemaphoreType.DMA((DEPTH,))]
    if not last:
        outs.append(pltpu.VMEM((rows, sub), BF16))
        scratch.append(pltpu.SemaphoreType.DMA)
    return pl.pallas_call(
        functools.partial(cross_kernel, start, last),
        in_specs=[vmem, pl.BlockSpec(memory_space=pl.ANY), vmem] + [vmem] * len(stats),
        out_specs=[vmem] * len(outs),
        out_shape=outs,
        scratch_shapes=scratch,
        compiler_params=pltpu.CompilerParams(vmem_limit_bytes=40 * MIB),
        cost_estimate=pl.CostEstimate(
            flops=8 * rows * cols * width, bytes_accessed=2 * rows * width, transcendentals=0
        ),
        name="cross",
    )(proj, act, ahead, *stats)


def combine_kernel(start, pieces, last, tokens, own_ref, got_ref, *refs):
    stat_refs, refs = refs[:pieces], refs[pieces:]
    if start:
        _, prev_ref, *refs = refs
    out_ref, gram_ref = refs
    cols = own_ref.shape[0]
    chunk = stat_refs[0].shape[1]
    nb = block_of(chunk, 1792)
    full = None
    for at in range(0, own_ref.shape[1], nb):
        piece, within = divmod(at, chunk)
        scale = stat_refs[piece][1:2, within : within + nb] * (1.0 / tokens)
        weighted = (own_ref[:, at : at + nb] + got_ref[:, at : at + nb]) * scale
        both = jnp.concatenate(halves(weighted), axis=0)
        out_ref[:, start + at : start + at + nb] = both
        square = lax.dot_general(both, both, NT, preferred_element_type=F32)
        full = square if full is None else full + square
    gram = (full[:cols, :cols] + full[cols:, cols:]) + (full[:cols, cols:] + full[cols:, :cols])
    packed = jnp.concatenate([gram[: cols // 2], gram[cols // 2 :]], axis=1)
    if start:
        packed = packed + prev_ref[...]
    if last:
        for r in range(gram_ref.shape[0]):
            gram_ref[r] = packed
    else:
        gram_ref[...] = packed


def combine(own, got, stats, start, whole, tokens, n, buffer, prev):
    cols, width = own.shape
    last = start + width == whole
    packed = (n, cols // 2, 2 * cols) if last else (cols // 2, 2 * cols)
    args = [own, got, *stats] + ([buffer, prev] if start else [])
    vmem = pl.BlockSpec(memory_space=pltpu.VMEM)
    return pl.pallas_call(
        functools.partial(combine_kernel, start, len(stats), last, tokens),
        in_specs=[vmem] * len(args),
        out_specs=[vmem, vmem],
        out_shape=[
            jax.ShapeDtypeStruct((2 * cols, whole), BF16),
            jax.ShapeDtypeStruct(packed, F32),
        ],
        input_output_aliases={len(args) - 2: 0} if start else {},
        compiler_params=pltpu.CompilerParams(vmem_limit_bytes=16 * MIB),
        cost_estimate=pl.CostEstimate(
            flops=8 * cols * cols * width, bytes_accessed=12 * cols * width, transcendentals=0
        ),
        name="combine",
    )(*args)


def inverse_factor(gram):
    cols = gram.shape[0]
    row = lax.broadcasted_iota(jnp.int32, (cols, cols), 0)
    lane = lax.broadcasted_iota(jnp.int32, (cols, cols), 1)
    diag = jnp.where(row == lane, gram, 0.0)
    down = lax.rsqrt(jnp.sum(diag, axis=1, keepdims=True))
    along = lax.rsqrt(jnp.sum(diag, axis=0, keepdims=True))
    gram = gram * down * along
    wide = jnp.concatenate([gram, (row == lane).astype(F32)], axis=1)
    tall = [wide[8 * b : 8 * b + 8] for b in range(cols // 8)]
    tile = tall[0].shape
    within = lax.broadcasted_iota(jnp.int32, tile, 0)

    def column(x, k):
        return jnp.broadcast_to(x[:, k : k + 1], tile)

    def line(x, i):
        return jnp.broadcast_to(x[i : i + 1], tile)

    def factors_of(a, b, c):
        over = 1.0 / (a * c - b * b)
        a, b, c = a * over, b * over, c * over
        return lambda x, y: (c * x - b * y, a * y - b * x)

    for at in range(cols // 8):
        base = 8 * at
        rows = [line(tall[at], j) for j in range(8)]
        below = range(at, cols // 8)
        columns = {t: [column(tall[t], base + j) for j in range(8)] for t in below}
        pivots = {(i, j): line(columns[at][j], i) for i in range(8) for j in range(i + 1)}
        change = {t: 0.0 for t in below}
        for z in range(0, 8, 2):
            factors = factors_of(pivots[z, z], pivots[z + 1, z], pivots[z + 1, z + 1])
            later = range(z + 2, 8)
            for t in below:
                first, second = factors(columns[t][z], columns[t][z + 1])
                for j in later:
                    columns[t][j] = columns[t][j] - (first * pivots[j, z] + second * pivots[j, z + 1])
                if t == at:
                    first = jnp.where(within > z + 1, first, 0.0)
                    second = jnp.where(within > z + 1, second, 0.0)
                change[t] = change[t] + (first * rows[z] + second * rows[z + 1])
            own = {i: factors(pivots[i, z], pivots[i, z + 1]) for i in later}
            for i in later:
                first, second = own[i]
                for j in range(z + 2, i + 1):
                    pivots[i, j] = pivots[i, j] - (first * pivots[j, z] + second * pivots[j, z + 1])
                rows[i] = rows[i] - (first * rows[z] + second * rows[z + 1])
        for t in below:
            tall[t] = tall[t] - change[t]
    wide = jnp.concatenate(tall, axis=0)
    diag = jnp.sum(jnp.where(row == lane, wide[:, :cols], 0.0), axis=1, keepdims=True)
    odd = row % 2 == 1
    beside = jnp.sum(jnp.where((row == lane + 1) & odd, wide[:, :cols], 0.0), axis=1, keepdims=True)
    above = pltpu.roll(wide, 1, 0)[:, cols:]
    diag_above = pltpu.roll(jnp.broadcast_to(diag, wide.shape), 1, 0)[:, 0:1]
    ratio = jnp.where(odd[:, 0:1], beside / diag_above, 0.0)
    unit = wide[:, cols:] - ratio * above
    return unit * lax.rsqrt(diag - ratio * beside) * along


def finish_kernel(nb, gram_ref, both_ref, out_ref, stage_ref, sem):
    cols = out_ref.shape[0]
    packed = jnp.sum(gram_ref[...], axis=0) / NEURONS
    gram = jnp.concatenate([packed[:, :cols], packed[:, cols:]], axis=0)
    head, rest = halves(inverse_factor(gram))
    twice = jnp.concatenate([head, head], axis=1)
    copies = []
    for s, at in enumerate(range(0, out_ref.shape[1], nb)):
        both = both_ref[:, at : at + nb]
        stage_ref[:, at : at + nb] = jnp.dot(twice, both, preferred_element_type=F32) + jnp.dot(
            rest, both[:cols], preferred_element_type=F32
        )
        copies.append(
            pltpu.make_async_copy(
                stage_ref.at[:, pl.ds(at, nb)], out_ref.at[:, pl.ds(at, nb)], sem.at[s]
            )
        )
        copies[-1].start()
    for copy in copies:
        copy.wait()


def finish(grams, both):
    cols, width = both.shape[0] // 2, both.shape[1]
    nb = block_of(width, FINAL)
    vmem = pl.BlockSpec(memory_space=pltpu.VMEM)
    return pl.pallas_call(
        functools.partial(finish_kernel, nb),
        in_specs=[vmem, vmem],
        out_specs=pl.BlockSpec(memory_space=pl.ANY),
        out_shape=jax.ShapeDtypeStruct((cols, width), F32),
        scratch_shapes=[pltpu.VMEM((cols, width), F32), pltpu.SemaphoreType.DMA((width // nb,))],
        compiler_params=pltpu.CompilerParams(vmem_limit_bytes=16 * MIB),
        name="finish",
    )(grams, both)


def local(activations, basis):
    tok_dev, neu_dev = activations.shape
    n, m = lax.axis_size("neuron"), lax.axis_size("token")
    tokens = tok_dev * m
    cols = basis.shape[1]
    basis_t = basis.T
    chunks = next(c for c in (CHUNKS, 7, 2, 1) if neu_dev % (128 * c) == 0)
    chunk = neu_dev // chunks

    own, got, stats = [], [], []
    part = buf = None
    peek = PEEK if DELAY > 1 and chunks > 1 else 0
    for step in range(chunks + DELAY):
        loads = step if step < chunks else None
        at = step - DELAY if step >= DELAY else None
        sums = (None, None) if at is None else (own[at], got[at])
        results = stream(
            tokens, chunk, activations, loads, buf, at, *sums, basis_t, part,
            at == chunks - 1, block_of(chunk, SUB) if at == chunks - 1 else 0,
            peek if step == 1 else 0, peek if step == 0 else 0,
        )
        if loads is not None:
            buf = results.pop(0)
            own.append(results.pop(0))
            got.append(swap_tokens(own[-1]))
        if at is not None:
            part = results.pop(0)
            stats.append(results.pop(0))
    (ahead,) = results

    blocks = part
    if tok_dev // n != ROWS:
        blocks = part.transpose(1, 0, 2).reshape(cols, n, tok_dev // n).transpose(1, 0, 2)
    blocks = lax.all_to_all(blocks, "neuron", 0, 0)
    block = sum(blocks[r].astype(F32) for r in range(n)).astype(BF16)
    blocks = jnp.broadcast_to(block[None], blocks.shape)
    proj = lax.all_to_all(blocks, "neuron", 0, 0)
    if proj.shape[2] % 128:
        proj = proj.transpose(1, 0, 2).reshape(1, cols, tok_dev)

    split = chunks - max(1, chunks // 4)
    spans = [(0, split), (split, chunks)] if split else [(0, chunks)]
    spans = [(lo * chunk, stats[lo:hi]) for lo, hi in spans]
    terms, swapped = [], []
    for start, stat in spans:
        term, *rest = cross(proj, activations, ahead, stat, start)
        ahead = rest[0] if rest else None
        terms.append(term)
        swapped.append(swap_tokens(term))
    both = gram = None
    for term, got, (start, stat) in zip(terms, swapped, spans):
        both, gram = combine(term, got, stat, start, neu_dev, tokens, n, both, gram)
    grams = lax.all_to_all(gram, "neuron", 0, 0)
    return finish(grams, both).T


def solution(mesh):
    placed = (P(("groups", "token"), "neuron"), P(("groups", "neuron"), None))
    return jax.shard_map(
        local, mesh=mesh, in_specs=placed, out_specs=P(("groups", "neuron"), None), check_vma=False
    )
```
